128 devices in a mesh: fsdp: 4 (over z), seq: 32 (over x, y, core).
Axes of the slice: x: 4, y: 4, z: 4, core: 2. Of those that a mesh axis runs over, the one named last changes fastest.
Arguments:
- queries: bfloat16 [4, 8192, 2048], P('fsdp', 'seq'), may hold values from -32 to 32
- keys: bfloat16 [4, 8192, 2048], P('fsdp', 'seq'), may hold values from -6 to 6
- values: bfloat16 [4, 8192, 2048], P('fsdp', 'seq'), may hold values from -6 to 6
- out_grad: bfloat16 [4, 8192, 2048], P('fsdp', 'seq'), may hold values from -6 to 6
- out_weight: bfloat16 [2048, 2048], P('fsdp'), may hold values from -0.125 to 0.125
- key_blocks: int32 [4, 64, 10], P('fsdp'), may hold values from 0 to 63, as said below
- block_counts: int32 [4, 64], P('fsdp'), may hold values from 2 to 10, as said below
Outputs:
- query_grad: bfloat16 [4, 8192, 2048], P('fsdp', 'seq')
- key_grad: bfloat16 [4, 8192, 2048], P('fsdp', 'seq')
- value_grad: bfloat16 [4, 8192, 2048], P('fsdp', 'seq')
- wo_grad: float32 [2048, 2048], P('fsdp')
The draws below stay inside these ranges and needn't reach their ends.
Inputs may be any that keep to these rules, and one draw needn't show every extreme that they name: `key_blocks`: within a row the numbers are distinct; slots 0, 1 and 2 hold blocks i, i + 1 and i - 1 modulo 64; slots at or past the row's count are ignored. `block_counts`: every sample has a query block whose count is 10.
All inputs are finite; a program needn't handle non-finite values.
Results may differ from the reference program's by a relative error of at most 0.025.
Values may be sent and summed in bfloat16 or wider, within the bound.
A program may use at most 128 MiB of HBM per device.

```python
import jax
import jax.numpy as jnp
from jax import lax

HEADS = 32
HD = 64
D = 2048
BLK = 128
MAXK = 10
SEQLEN = 8192
NBLK = 64
BATCH = 4


def base_field(key):
    return jax.random.truncated_normal(jax.random.fold_in(key, 11), -6.0, 6.0, (BATCH, SEQLEN, D), jnp.float32)


def draw_queries(key, part):
    field = base_field(jax.random.fold_in(key, 1))
    return field.astype(jnp.bfloat16)


def draw_keys(key, part):
    field = base_field(jax.random.fold_in(key, 2))
    return field.astype(jnp.bfloat16)


def draw_key_blocks(key, part):
    row_keys = jax.random.split(jax.random.fold_in(key, 5), BATCH * NBLK)

    def one_row(row_key):
        others = jax.random.permutation(row_key, jnp.arange(2, NBLK - 1, dtype=jnp.int32))
        return jnp.concatenate([jnp.array([0, 1, NBLK - 1], jnp.int32), others[:MAXK - 3].astype(jnp.int32)])
    offsets = jax.vmap(one_row)(row_keys).reshape(BATCH, NBLK, MAXK)
    own = jnp.arange(NBLK, dtype=jnp.int32)[None, :, None]
    return ((own + offsets) % NBLK).astype(jnp.int32)


def draw_block_counts(key, part):
    counts = jax.random.randint(jax.random.fold_in(key, 3), (BATCH, NBLK), 2, MAXK + 1)
    fullest = jax.random.randint(jax.random.fold_in(key, 4), (BATCH, 1), 0, NBLK)
    return jnp.where(jnp.arange(NBLK)[None, :] == fullest, MAXK, counts).astype(jnp.int32)


def steps_of(rng, extent, cuts, least, top_value):
    gain, own = 1.0, jax.random.fold_in(rng, 6)
    for position, blocks in cuts:
        steps = jnp.exp(jax.random.uniform(jax.random.fold_in(own, position), (blocks,), jnp.float32, least / len(cuts), top_value / len(cuts)))
        gain = gain * jnp.repeat(steps, extent[position] // blocks).reshape([-1 if axis == position else 1 for axis in range(len(extent))])
    return gain


def gaussian(rng, extent, deviation, limit, cuts=(), held_as=jnp.bfloat16):
    values = jax.random.normal(rng, extent, jnp.float32) * deviation
    if len(cuts) > 0:
        values = steps_of(rng, extent, cuts, -0.22, 0.18) * values
    return jnp.clip(values, min=-limit, max=limit).astype(held_as)


def setup_inputs(seed: int = 0) -> dict:
    seeds = jax.random.split(jax.random.key(seed), 8)
    queries = draw_queries(jax.random.fold_in(seeds[7], 71), 0)
    keys = draw_keys(jax.random.fold_in(seeds[7], 71), 0)
    values = gaussian(seeds[2], (BATCH, SEQLEN, D), 1.0, 6.0, ((0, 4), (1, 32)))
    out_grad = gaussian(seeds[3], (BATCH, SEQLEN, D), 1.0, 6.0, ((0, 4), (1, 32)))
    out_weight = gaussian(seeds[4], (D, D), D ** -0.5, 0.125, ((0, 4),))
    key_blocks = draw_key_blocks(jax.random.fold_in(seeds[7], 71), 0)
    block_counts = draw_block_counts(jax.random.fold_in(seeds[7], 71), 0)
    return dict(queries=queries, keys=keys, values=values, out_grad=out_grad, out_weight=out_weight, key_blocks=key_blocks, block_counts=block_counts)


NEG_FILL = -1e30


def attend_head(query_h, key_h, value_h, grad_h, adjacency, counts):
    scale_factor = HD ** -0.5
    keys_taken = key_h[adjacency].astype(jnp.float32)
    values_taken = value_h[adjacency].astype(jnp.float32)
    slot_live = jnp.arange(MAXK)[None, :] < counts[:, None]
    usable = slot_live[:, None, :, None]
    query_full = query_h.astype(jnp.float32)
    grad_full = grad_h.astype(jnp.float32)
    score = jnp.einsum('iqd,ijkd->iqjk', query_full, keys_taken) * scale_factor
    score = jnp.where(usable, score, NEG_FILL)
    row_max = jnp.max(score, axis=(2, 3))
    expo = jnp.where(usable, jnp.exp(score - row_max[:, :, None, None]), 0.0)
    row_sum = jnp.sum(expo, axis=(2, 3))
    prob_full = expo / row_sum[:, :, None, None]
    prob_half = prob_full.astype(jnp.bfloat16)
    attn_out = jnp.einsum('iqjk,ijkd->iqd', prob_half.astype(jnp.float32), values_taken).astype(jnp.bfloat16)
    row_dot = jnp.sum(grad_full * attn_out.astype(jnp.float32), axis=-1)
    prob_grad = jnp.einsum('iqd,ijkd->iqjk', grad_full, values_taken)
    score_grad = (prob_full * (prob_grad - row_dot[:, :, None, None])).astype(jnp.bfloat16)
    score_wide = score_grad.astype(jnp.float32)
    query_grad = (jnp.einsum('iqjk,ijkd->iqd', score_wide, keys_taken) * scale_factor).astype(jnp.bfloat16)
    key_terms = jnp.einsum('iqjk,iqd->ijkd', score_wide, query_full) * scale_factor
    key_grad = jnp.zeros((NBLK, BLK, HD), jnp.float32).at[adjacency].add(key_terms).astype(jnp.bfloat16)
    value_terms = jnp.einsum('iqjk,iqd->ijkd', prob_half.astype(jnp.float32), grad_full)
    value_grad = jnp.zeros((NBLK, BLK, HD), jnp.float32).at[adjacency].add(value_terms).astype(jnp.bfloat16)
    return query_grad, key_grad, value_grad, attn_out


def split_heads(array):
    return array.reshape(NBLK, BLK, HEADS, HD).transpose(2, 0, 1, 3)


def merge_heads(array):
    return array.transpose(1, 2, 0, 3).reshape(SEQLEN, D)


def reference(queries, keys, values, out_grad, out_weight, key_blocks, block_counts):
    attn_grad = jnp.dot(out_grad.reshape(-1, D), out_weight.T, preferred_element_type=jnp.float32)
    attn_grad = attn_grad.astype(jnp.bfloat16).reshape(BATCH, SEQLEN, D)

    def one_sample(packed):
        query_s, key_s, value_s, grad_s, adjacency, counts = packed

        def one_head(heads_in):
            return attend_head(heads_in[0], heads_in[1], heads_in[2], heads_in[3], adjacency, counts)

        results = lax.map(one_head, (split_heads(query_s), split_heads(key_s), split_heads(value_s), split_heads(grad_s)))
        return tuple(merge_heads(result) for result in results)

    query_grad, key_grad, value_grad, attn_out = lax.map(one_sample, (queries, keys, values, attn_grad, key_blocks, block_counts))
    wo_grad = jnp.dot(attn_out.reshape(-1, D).T, out_grad.reshape(-1, D), preferred_element_type=jnp.float32)
    return query_grad, key_grad, value_grad, wo_grad
```

```python
import jax
import jax.numpy as jnp
from jax import lax
from jax.experimental import pallas as pl
from jax.experimental.pallas import tpu as pltpu
from jax.sharding import PartitionSpec as P

HEADS = 32
HD = 64
BLK = 128
MAXK = 10
LOG2E = 1.4426950408889634


def attention_kernel(adj_ref, count_ref, qg_ref, kv_ref, dqo_ref, dkv_ref, acc_ref, kvt_ref, sd_ref, te_ref):
    blocks = qg_ref.shape[0] // BLK
    lane = lax.broadcasted_iota(jnp.int32, (BLK, BLK), 1)
    first = lane < HD
    half_scale = jnp.where(first, HD ** -0.5, 1.0).astype(jnp.float32)
    score_scale = HD ** -0.5 * LOG2E

    def rows(b):
        return pl.ds(pl.multiple_of(b * BLK, BLK), BLK)

    @pl.loop(0, blocks)
    def _(b):
        acc_ref[rows(b), :] = jnp.zeros((BLK, BLK), jnp.float32)
        kvt_ref[rows(b), :] = kv_ref[rows(b), :].T

    def fold(x, op):
        parts = [x[r * 8:(r + 1) * 8] for r in range(x.shape[0] // 8)]
        while len(parts) > 1:
            parts = [op(parts[t], parts[t + 1]) for t in range(0, len(parts) - 1, 2)] + (
                [parts[-1]] if len(parts) % 2 else [])
        return parts[0]

    def one_block(i, n):
        qg = qg_ref[rows(i), :]
        zero = jnp.zeros_like(qg)
        pair = jnp.concatenate([jnp.where(first, qg, zero), jnp.where(first, zero, qg)], axis=0)
        picked = [adj_ref[i, j] for j in range(n)]
        top = None
        for j in range(n):
            sd = lax.dot_general(
                kv_ref[rows(picked[j]), :], pair, (((1,), (1,)), ((), ())),
                preferred_element_type=jnp.float32)
            sd_ref[j * BLK:(j + 1) * BLK, :] = sd
            part = fold(sd[:, :BLK], jnp.maximum)
            top = part if top is None else jnp.maximum(top, part)
        top = jnp.max(top, axis=0, keepdims=True) * score_scale
        total = None
        dots = None
        for j in range(n):
            at = slice(j * BLK, (j + 1) * BLK)
            expo = jnp.exp2(sd_ref[at, :BLK] * score_scale - top)
            sd_ref[at, :BLK] = expo
            part = fold(expo, jnp.add)
            total = part if total is None else total + part
            part = fold(expo * sd_ref[at, BLK:], jnp.add)
            dots = part if dots is None else dots + part
        inv = 1.0 / jnp.sum(total, axis=0, keepdims=True)
        row_dot = jnp.sum(dots, axis=0, keepdims=True) * inv
        out = None
        for j in range(n):
            at = slice(j * BLK, (j + 1) * BLK)
            prob = sd_ref[at, :BLK] * inv
            grad = prob * (sd_ref[at, BLK:] - row_dot)
            te = jnp.concatenate([grad.astype(jnp.bfloat16), prob.astype(jnp.bfloat16)], axis=1)
            te_ref[at, :] = te
            acc_ref[rows(picked[j]), :] += jnp.dot(te, pair, preferred_element_type=jnp.float32)
        kvt = jnp.concatenate([kvt_ref[rows(picked[j]), :] for j in range(n)], axis=1)
        out = jnp.dot(kvt, te_ref[:n * BLK, :], preferred_element_type=jnp.float32)
        both = jnp.concatenate([out[:HD, :BLK], out[HD:, BLK:]], axis=0).T
        dqo_ref[rows(i), :] = (both * half_scale).astype(jnp.bfloat16)

    @pl.loop(0, blocks)
    def _(i):
        count = count_ref[i]
        for n in range(2, MAXK + 1):
            @pl.when(count == n)
            def _():
                one_block(i, n)

    @pl.loop(0, blocks)
    def _(b):
        dkv_ref[rows(b), :] = (acc_ref[rows(b), :] * half_scale).astype(jnp.bfloat16)


def attention(adjacency, counts, qg, kv):
    tokens = qg.shape[0]
    whole = pl.BlockSpec(memory_space=pltpu.VMEM)
    scalar = pl.BlockSpec(memory_space=pltpu.SMEM)
    shape = jax.ShapeDtypeStruct((tokens, 2 * HD), jnp.bfloat16)
    return pl.pallas_call(
        attention_kernel,
        out_shape=(shape, shape),
        in_specs=[scalar, scalar, whole, whole],
        out_specs=(whole, whole),
        scratch_shapes=[
            pltpu.VMEM((tokens, 2 * HD), jnp.float32),
            pltpu.VMEM((tokens, 2 * HD), jnp.bfloat16),
            pltpu.VMEM((MAXK * BLK, 2 * BLK), jnp.float32),
            pltpu.VMEM((MAXK * BLK, 2 * BLK), jnp.bfloat16),
        ],
        compiler_params=pltpu.CompilerParams(vmem_limit_bytes=48 << 20),
    )(adjacency, counts, qg, kv)


def pack_kernel(left_ref, right_ref, out_ref):
    for j in range(HEADS // 2):
        at = slice(j * 2 * HD, (j + 1) * 2 * HD)
        left, right = left_ref[:, at], right_ref[:, at]
        out_ref[2 * j] = jnp.concatenate([left[:, :HD], right[:, :HD]], axis=1)
        out_ref[2 * j + 1] = jnp.concatenate([left[:, HD:], right[:, HD:]], axis=1)


def pack(left, right):
    whole = pl.BlockSpec(memory_space=pltpu.VMEM)
    return pl.pallas_call(
        pack_kernel,
        out_shape=jax.ShapeDtypeStruct((HEADS, left.shape[0], 2 * HD), left.dtype),
        in_specs=[whole, whole],
        out_specs=whole,
    )(left, right)


def unpack_kernel(in_ref, left_ref, right_ref):
    for j in range(HEADS // 2):
        at = slice(j * 2 * HD, (j + 1) * 2 * HD)
        one, two = in_ref[2 * j], in_ref[2 * j + 1]
        left_ref[:, at] = jnp.concatenate([one[:, :HD], two[:, :HD]], axis=1)
        right_ref[:, at] = jnp.concatenate([one[:, HD:], two[:, HD:]], axis=1)


def unpack(packed):
    whole = pl.BlockSpec(memory_space=pltpu.VMEM)
    shape = jax.ShapeDtypeStruct((packed.shape[1], HEADS * HD), packed.dtype)
    return pl.pallas_call(
        unpack_kernel,
        out_shape=(shape, shape),
        in_specs=[whole],
        out_specs=(whole, whole),
    )(packed)


def exchange(packed):
    return lax.all_to_all(packed, "seq", split_axis=0, concat_axis=0, tiled=True)


def on_device(queries, keys, values, out_grad, out_weight, key_blocks, block_counts):
    local_tokens, width = queries.shape[1:]
    parts = lax.axis_size("seq")
    loss_grad = out_grad[0]
    kv = exchange(pack(keys[0], values[0])).reshape(-1, 2 * HD)
    attn_grad = lax.dot_general(
        loss_grad,
        lax.all_gather(out_weight, "fsdp", axis=0, tiled=True),
        (((1,), (1,)), ((), ())),
        preferred_element_type=jnp.float32,
    ).astype(jnp.bfloat16)
    qg = exchange(pack(queries[0], attn_grad)).reshape(-1, 2 * HD)
    dqo, dkv = attention(key_blocks[0], block_counts[0], qg, kv)
    query_grad, attn_out = unpack(exchange(dqo.reshape(parts, local_tokens, 2 * HD)))
    term = lax.dot_general(
        attn_out, loss_grad, (((0,), (0,)), ((), ())), preferred_element_type=jnp.float32
    ).astype(jnp.bfloat16)
    planes = lax.axis_size("fsdp")
    term = term.reshape(planes, parts, width // planes // parts, width).transpose(1, 0, 2, 3)
    term = lax.all_to_all(term, "seq", split_axis=0, concat_axis=0, tiled=True)
    term = jnp.sum(term.astype(jnp.float32), axis=0).astype(jnp.bfloat16)
    term = lax.all_to_all(term, "fsdp", split_axis=0, concat_axis=0, tiled=True)
    share = jnp.sum(term.astype(jnp.float32), axis=0)
    wo_grad = lax.all_gather(share.astype(jnp.bfloat16), "seq", axis=0, tiled=True).astype(jnp.float32)
    key_grad, value_grad = unpack(exchange(dkv.reshape(parts, local_tokens, 2 * HD)))
    return (query_grad[None], key_grad[None], value_grad[None], wo_grad)


def solution(mesh):
    return jax.shard_map(
        on_device,
        mesh=mesh,
        in_specs=(
            P("fsdp", "seq", None),
            P("fsdp", "seq", None),
            P("fsdp", "seq", None),
            P("fsdp", "seq", None),
            P("fsdp", None),
            P("fsdp", None, None),
            P("fsdp", None),
        ),
        out_specs=(
            P("fsdp", "seq", None),
            P("fsdp", "seq", None),
            P("fsdp", "seq", None),
            P("fsdp", None),
        ),
        check_vma=False,
    )
```

```python
import jax
import jax.numpy as jnp
from jax import lax
from jax.experimental import pallas as pl
from jax.experimental.pallas import tpu as pltpu
from jax.sharding import PartitionSpec as P

HEADS = 32
HD = 64
BLK = 128
MAXK = 10
LOG2E = 1.4426950408889634
SEQ = 32
SIDE = 4
CHIPS = 16
PLANES = 4
D = 2048
ROWS = 256
BF = jnp.bfloat16
F32 = jnp.float32
PARTS = ((0, 768), (768, 640), (1408, 640))


def remote(src, dst, send_sem, recv_sem, **where):
    return pltpu.make_async_remote_copy(
        src_ref=src, dst_ref=dst, send_sem=send_sem, recv_sem=recv_sem,
        device_id=where, device_id_type=pl.DeviceIdType.MESH)


def local(src, dst, sem):
    return pltpu.make_async_copy(src, dst, sem)


def position():
    plane, member = lax.axis_index("fsdp"), lax.axis_index("seq")
    chip, core = lax.div(member, 2), lax.rem(member, 2)
    return plane, member, chip, core, lax.div(chip, SIDE), lax.rem(chip, SIDE)


def entry_barrier(plane, member):
    barrier = pltpu.get_barrier_semaphore()

    @pl.loop(1, SEQ)
    def _(k):
        pl.semaphore_signal(
            barrier, inc=1, device_id={"seq": lax.rem(member + k, SEQ)},
            device_id_type=pl.DeviceIdType.MESH)

    @pl.loop(1, PLANES)
    def _(k):
        pl.semaphore_signal(
            barrier, inc=1, device_id={"fsdp": lax.rem(plane + k, PLANES)},
            device_id_type=pl.DeviceIdType.MESH)

    pl.semaphore_wait(barrier, SEQ + PLANES - 2)


def halves(one, two):
    return (jnp.concatenate([one[:, :HD], two[:, :HD]], axis=1),
            jnp.concatenate([one[:, HD:], two[:, HD:]], axis=1))


def head_kernel(q_ref, k_ref, v_ref, og_ref, w_ref, q_out, kv_out, g_out, both_out,
                q_pack, kv_pack, g_pack, both_ref, w_buf,
                q_send, kv_send, g_send, q_recv, kv_recv, g_recv,
                w_send, w_recv, w_own, both_send, both_recv, both_own):
    plane, member, chip, core, _, _ = position()
    up, down = lax.rem(plane + 1, PLANES), lax.rem(plane + 3, PLANES)
    far = lax.rem(plane + 2, PLANES)
    sibling = chip * 2 + 1 - core
    mine = pl.ds(pl.multiple_of(core * ROWS, ROWS), ROWS)
    w_mine = local(w_ref.at[mine], w_buf.at[plane], w_own.at[0])
    w_mine.start()
    both_mine = local(og_ref, both_ref.at[mine], w_own.at[1])
    both_mine.start()
    entry_barrier(plane, member)
    w_up = remote(w_ref.at[mine], w_buf.at[plane], w_send.at[0], w_recv.at[0], fsdp=up)
    w_down = remote(w_ref.at[mine], w_buf.at[plane], w_send.at[1], w_recv.at[1], fsdp=down)
    w_up.start()
    w_down.start()
    both_copy = remote(og_ref, both_ref.at[mine], both_send, both_recv, seq=sibling)
    both_copy.start()

    def send(block, head, out, slot, send_sem, recv_sem):
        @pl.when(head != member)
        def _():
            remote(block, out.at[slot], send_sem, recv_sem, seq=head).start()

        @pl.when(head == member)
        def _():
            local(block, out.at[slot], recv_sem).start()

    def sent(block, head, out, slot, send_sem, recv_sem):
        @pl.when(head != member)
        def _():
            remote(block, out.at[slot], send_sem, recv_sem, seq=head).wait_send()

    @pl.loop(0, CHIPS)
    def _(k):
        j = lax.rem(chip + k, CHIPS)
        at = pl.ds(pl.multiple_of(j * 2 * HD, 2 * HD), 2 * HD)
        kv = halves(k_ref[:, at], v_ref[:, at])
        for e in range(2):
            kv_pack[2 * j + e] = kv[e]
            send(kv_pack.at[2 * j + e], 2 * j + e, kv_out, member, kv_send.at[2 * j + e], kv_recv)

    @pl.loop(0, CHIPS)
    def _(k):
        j = lax.rem(chip + k, CHIPS)
        at = pl.ds(pl.multiple_of(j * 2 * HD, 2 * HD), 2 * HD)
        q = halves(q_ref[:BLK, at], q_ref[BLK:, at])
        for e in range(2):
            q_pack[2 * j + e] = q[e]
            send(q_pack.at[2 * j + e], 2 * j + e, q_out, member, q_send.at[2 * j + e], q_recv)

    def project(which):
        for pair in range(2):
            grad = lax.dot_general(
                both_ref[...], w_buf[which, pair * BLK:(pair + 1) * BLK, :],
                (((1,), (1,)), ((), ())), preferred_element_type=F32).astype(BF)
            top = halves(grad[:BLK], grad[BLK:2 * BLK])
            low = halves(grad[2 * BLK:3 * BLK], grad[3 * BLK:])
            for e in range(2):
                slot = which * SIDE + pair * 2 + e
                head = which * 2 * SIDE + core * SIDE + pair * 2 + e
                g_pack[slot, :BLK, :] = top[e]
                g_pack[slot, BLK:, :] = low[e]
                send(g_pack.at[slot], head, g_out, chip, g_send.at[slot], g_recv)

    w_mine.wait()
    both_mine.wait()
    both_copy.wait()
    both_write = local(both_ref, both_out, both_own)
    both_write.start()
    project(plane)
    w_up.wait()
    first = pl.ds(0, BLK)
    second = pl.ds(BLK, BLK)
    pass_up = remote(w_buf.at[down, first], w_buf.at[down, first], w_send.at[2], w_recv.at[2], fsdp=up)
    pass_up.start()
    w_down.wait()
    pass_down = remote(w_buf.at[up, second], w_buf.at[up, second], w_send.at[3], w_recv.at[3], fsdp=down)
    pass_down.start()
    project(down)
    project(up)
    pass_up.wait()
    pass_down.wait()
    project(far)
    both_write.wait()

    @pl.loop(0, SEQ)
    def _(d):
        sent(kv_pack.at[d], d, kv_out, member, kv_send.at[d], kv_recv)
        sent(q_pack.at[d], d, q_out, member, q_send.at[d], q_recv)

    @pl.loop(0, CHIPS)
    def _(slot):
        head = lax.div(slot, SIDE) * 2 * SIDE + core * SIDE + lax.rem(slot, SIDE)
        sent(g_pack.at[slot], head, g_out, chip, g_send.at[slot], g_recv)

    local(kv_out, kv_out, kv_recv).wait()
    local(q_out, q_out, q_recv).wait()
    local(g_out, g_out, g_recv).wait()


def head_exchange(queries, keys, values, out_grad, out_weight):
    anyway = pl.BlockSpec(memory_space=pl.ANY)
    whole = pl.BlockSpec(memory_space=pltpu.VMEM)
    dma = pltpu.SemaphoreType.DMA
    return pl.pallas_call(
        head_kernel,
        out_shape=(
            jax.ShapeDtypeStruct((SEQ, BLK, 2 * HD), BF),
            jax.ShapeDtypeStruct((SEQ, ROWS, 2 * HD), BF),
            jax.ShapeDtypeStruct((CHIPS, ROWS, 2 * HD), BF),
            jax.ShapeDtypeStruct((2 * ROWS, D), BF),
        ),
        in_specs=[whole, whole, whole, whole, anyway],
        out_specs=(anyway, anyway, anyway, anyway),
        scratch_shapes=[
            pltpu.VMEM((SEQ, BLK, 2 * HD), BF),
            pltpu.VMEM((SEQ, ROWS, 2 * HD), BF),
            pltpu.VMEM((CHIPS, ROWS, 2 * HD), BF),
            pltpu.VMEM((2 * ROWS, D), BF),
            pltpu.VMEM((PLANES, ROWS, D), BF),
            dma((SEQ,)), dma((SEQ,)), dma((CHIPS,)), dma, dma, dma,
            dma((4,)), dma((4,)), dma((2,)), dma, dma, dma,
        ],
        compiler_params=pltpu.CompilerParams(
            collective_id=0, has_side_effects=True, vmem_limit_bytes=48 << 20),
    )(queries, keys, values, out_grad, out_weight)


def tail_kernel(ot_ref, dq_ref, dkv_ref, both_ref, dq_out, dkv_out, wo_out,
                o_buf, own_buf, *rest):
    bufs = [rest[6 * t:6 * t + 6] for t in range(3)]
    (o_send, dq_send, dkv_send, o_recv, dq_recv, dkv_recv, step_send, step_recv,
     wo_send, wo_recv, wo_own, pass_send, pass_recv) = rest[18:]
    plane, member, chip, core, x, y = position()
    entry_barrier(plane, member)
    target = lax.rem(lax.div(member, SIDE), 2)
    slot = lax.div(member, 2 * SIDE) * SIDE + lax.rem(member, SIDE)

    def o_copy(q):
        at = pl.ds(pl.multiple_of(q * 2 * ROWS, 2 * ROWS), 2 * ROWS)
        return ot_ref.at[:, at], o_buf.at[slot]

    @pl.loop(0, CHIPS)
    def _(k):
        q = lax.rem(chip + k, CHIPS)
        to = q * 2 + target
        src, dst = o_copy(q)

        @pl.when(to != member)
        def _():
            remote(src, dst, o_send.at[q], o_recv, seq=to).start()

        @pl.when(to == member)
        def _():
            local(src, dst, o_recv).start()

    local(dq_ref.at[member], dq_out.at[member], dq_recv).start()
    local(dkv_ref.at[member], dkv_out.at[member], dkv_recv).start()

    @pl.loop(1, SEQ)
    def _(k):
        to = lax.rem(member + k, SEQ)
        remote(dkv_ref.at[to], dkv_out.at[member], dkv_send.at[to], dkv_recv, seq=to).start()
        remote(dq_ref.at[to], dq_out.at[member], dq_send.at[to], dq_recv, seq=to).start()

    local(o_buf, o_buf, o_recv).wait()

    def place(part, zq, value, at):
        buf = bufs[part][0]
        if part == 0:
            buf[zq, :, at] = value
            return
        for xq in range(SIDE):
            for yq in range(SIDE):
                piece = value[(xq * SIDE + yq) * 16:(xq * SIDE + yq + 1) * 16]
                if part == 1:
                    buf[xq, pl.ds(pl.multiple_of(yq * 64 + zq * 16, 16), 16), at] = piece
                else:
                    buf[yq, pl.ds(pl.multiple_of(zq * 64 + xq * 16, 16), 16), at] = piece

    axes = (("fsdp", plane), ("x", x), ("y", y))
    orders = ((0, 1, 2), (1, 2, 0), (2, 0, 1))

    def steps(part, stage):
        name, here = axes[orders[part][stage]]
        send_buf, recv_buf = bufs[part][2 * stage], bufs[part][2 * stage + 1]
        copies = []
        for k in range(1, SIDE):
            there = lax.rem(here + k, SIDE)
            if name == "fsdp":
                where = dict(fsdp=there)
            elif name == "x":
                where = dict(seq=(there * SIDE + y) * 2 + core)
            else:
                where = dict(seq=(x * SIDE + there) * 2 + core)
            copies.append(remote(
                send_buf.at[there], recv_buf.at[here],
                step_send.at[part, stage, k - 1], step_recv.at[part, stage, k - 1], **where))
        return copies, here, send_buf, recv_buf

    def start(part, stage):
        for copy in steps(part, stage)[0]:
            copy.start()

    def multiply(tiles, parts_of):
        @pl.loop(0, PLANES)
        def _(zq):
            lhs = o_buf[pl.ds(zq * SIDE, SIDE)].reshape(ROWS, 2 * ROWS)
            for tile in tiles:
                value = jnp.dot(
                    lhs, both_ref[:, tile * ROWS:(tile + 1) * ROWS],
                    preferred_element_type=F32).astype(BF)
                for half in range(2):
                    col = tile * ROWS + half * BLK
                    for part in parts_of:
                        base, width = PARTS[part]
                        if base <= col < base + width:
                            place(part, zq, value[:, half * BLK:(half + 1) * BLK],
                                  slice(col - base, col - base + BLK))

    multiply((0, 1, 2), (0,))
    start(0, 0)
    multiply((3, 4, 5), (1, 2))
    start(1, 0)
    multiply((6, 7), (2,))
    start(2, 0)

    for stage in range(3):
        for part in range(3):
            copies, here, send_buf, recv_buf = steps(part, stage)
            for copy in copies:
                copy.wait_recv()
            base, width = PARTS[part]
            rows = send_buf.shape[1]
            total = None
            for piece in range(max(1, rows // 64)):
                count = min(rows, 64)
                at = pl.ds(piece * count, count)
                total = send_buf[here, at, :].astype(F32)
                for k in range(1, SIDE):
                    total = total + recv_buf[lax.rem(here + k, SIDE), at, :].astype(F32)
                if stage == 2:
                    own_buf[:, base:base + width] = total.astype(BF)
                else:
                    next_buf = bufs[part][2 * stage + 2]
                    if rows == 256:
                        next_buf[piece] = total.astype(BF)
                    else:
                        for t in range(SIDE):
                            next_buf[t] = total[t * 16:(t + 1) * 16].astype(BF)
            if stage < 2:
                start(part, stage + 1)

    def wo_rows(which, q):
        return wo_out.at[pl.ds(pl.multiple_of((which * CHIPS + q) * 16, 16), 16)]

    sibling = chip * 2 + 1 - core
    own = local(own_buf, wo_rows(core, chip), wo_own)
    own.start()

    @pl.loop(1, CHIPS)
    def _(k):
        q = lax.rem(chip + k, CHIPS)
        remote(own_buf, wo_rows(core, chip), wo_send.at[q], wo_recv.at[chip], seq=q * 2 + core).start()

    first = remote(own_buf, wo_rows(core, chip), pass_send.at[chip], pass_recv, seq=sibling)
    first.start()

    @pl.loop(1, CHIPS)
    def _(k):
        q = lax.rem(chip + CHIPS - k, CHIPS)
        remote(own_buf, wo_rows(core, q), wo_send.at[q], wo_recv.at[q], seq=q * 2 + core).wait_recv()
        remote(wo_rows(core, q), wo_rows(core, q), pass_send.at[q], pass_recv, seq=sibling).start()

    own.wait()
    other = pl.ds(pl.multiple_of((1 - core) * ROWS, ROWS), ROWS)
    local(wo_out.at[other], wo_out.at[other], pass_recv).wait()
    first.wait_send()

    @pl.loop(1, CHIPS)
    def _(k):
        q = lax.rem(chip + k, CHIPS)
        remote(own_buf, wo_rows(core, chip), wo_send.at[q], wo_recv.at[chip], seq=q * 2 + core).wait_send()
        remote(wo_rows(core, q), wo_rows(core, q), pass_send.at[q], pass_recv, seq=sibling).wait_send()

    @pl.loop(0, CHIPS)
    def _(q):
        to = q * 2 + target
        src, dst = o_copy(q)

        @pl.when(to != member)
        def _():
            remote(src, dst, o_send.at[q], o_recv, seq=to).wait_send()

    for stage in range(3):
        for part in range(3):
            for copy in steps(part, stage)[0]:
                copy.wait_send()

    @pl.loop(1, SEQ)
    def _(k):
        to = lax.rem(member + k, SEQ)
        remote(dkv_ref.at[to], dkv_out.at[member], dkv_send.at[to], dkv_recv, seq=to).wait_send()
        remote(dq_ref.at[to], dq_out.at[member], dq_send.at[to], dq_recv, seq=to).wait_send()

    local(dkv_out, dkv_out, dkv_recv).wait()
    local(dq_out, dq_out, dq_recv).wait()


def tail_exchange(ot, dq, dkv, both):
    anyway = pl.BlockSpec(memory_space=pl.ANY)
    whole = pl.BlockSpec(memory_space=pltpu.VMEM)
    dma = pltpu.SemaphoreType.DMA
    stages = []
    for _, width in PARTS:
        for rows in (256, 64, 16):
            stages += [pltpu.VMEM((SIDE, rows, width), BF)] * 2
    return pl.pallas_call(
        tail_kernel,
        out_shape=(
            jax.ShapeDtypeStruct((SEQ, BLK, 2 * HD), BF),
            jax.ShapeDtypeStruct((SEQ, ROWS, 2 * HD), BF),
            jax.ShapeDtypeStruct((2 * ROWS, D), BF),
        ),
        in_specs=[anyway, anyway, anyway, whole],
        out_specs=(anyway, anyway, anyway),
        scratch_shapes=[
            pltpu.VMEM((CHIPS, HD, 2 * ROWS), BF),
            pltpu.VMEM((16, D), BF),
            *stages,
            dma((CHIPS,)), dma((SEQ,)), dma((SEQ,)), dma, dma, dma,
            dma((3, 3, 3)), dma((3, 3, 3)),
            dma((CHIPS,)), dma((CHIPS,)), dma, dma((CHIPS,)), dma,
        ],
        compiler_params=pltpu.CompilerParams(
            collective_id=1, has_side_effects=True, vmem_limit_bytes=48 << 20),
    )(ot, dq, dkv, both)


def finish_kernel(dq_ref, dkv_ref, wo_ref, dq_out, dk_out, dv_out, wo_out):
    for j in range(HEADS // 2):
        at = slice(j * 2 * HD, (j + 1) * 2 * HD)
        one, two = dkv_ref[2 * j], dkv_ref[2 * j + 1]
        dk_out[:, at], dv_out[:, at] = halves(one, two)
        one, two = dq_ref[2 * j], dq_ref[2 * j + 1]
        dq_out[:BLK, at], dq_out[BLK:, at] = halves(one, two)
    for r in range(8):
        at = slice(r * 64, (r + 1) * 64)
        wo_out[at, :] = wo_ref[at, :].astype(F32)


def finish(dq, dkv, wo):
    whole = pl.BlockSpec(memory_space=pltpu.VMEM)
    shape = jax.ShapeDtypeStruct((ROWS, D), BF)
    return pl.pallas_call(
        finish_kernel,
        out_shape=(shape, shape, shape, jax.ShapeDtypeStruct(wo.shape, F32)),
        in_specs=[whole] * 3,
        out_specs=(whole,) * 4,
        compiler_params=pltpu.CompilerParams(vmem_limit_bytes=48 << 20),
    )(dq, dkv, wo)


def attention_kernel(adj_ref, count_ref, q_ref, g_ref, kv_ref, dq_ref, ot_ref, dkv_ref,
                     qg_ref, acc_ref, kvt_ref, dqt_ref, sd_ref, te_ref):
    blocks = kv_ref.shape[0] // BLK
    first = lax.broadcasted_iota(jnp.int32, (BLK, BLK), 1) < HD
    half_scale = jnp.where(first, HD ** -0.5, 1.0).astype(F32)
    score_scale = HD ** -0.5 * LOG2E

    def rows(b):
        return pl.ds(pl.multiple_of(b * BLK, BLK), BLK)

    def swap(value):
        return jnp.concatenate([value[:, HD:], value[:, :HD]], axis=1)

    @pl.loop(0, blocks)
    def _(b):
        acc_ref[rows(b), :] = jnp.zeros((BLK, BLK), F32)
        kvt_ref[rows(b), :] = kv_ref[rows(b), :].T

    @pl.loop(0, blocks // 2)
    def _(b):
        q, g = q_ref[rows(b), :], g_ref[rows(b), :]
        qg_ref[rows(2 * b), :] = jnp.where(first, q, swap(g))
        qg_ref[rows(2 * b + 1), :] = jnp.where(first, swap(q), g)

    def fold(value, op):
        parts = [value[r * 8:(r + 1) * 8] for r in range(value.shape[0] // 8)]
        while len(parts) > 1:
            parts = [op(parts[t], parts[t + 1]) for t in range(0, len(parts) - 1, 2)] + (
                [parts[-1]] if len(parts) % 2 else [])
        return parts[0]

    def one_block(i, n):
        qg = qg_ref[rows(i), :]
        zero = jnp.zeros_like(qg)
        pair = jnp.concatenate([jnp.where(first, qg, zero), jnp.where(first, zero, qg)], axis=0)
        picked = [adj_ref[i, j] for j in range(n)]
        top = None
        for j in range(n):
            sd = lax.dot_general(
                kv_ref[rows(picked[j]), :], pair, (((1,), (1,)), ((), ())),
                preferred_element_type=F32)
            sd_ref[j * BLK:(j + 1) * BLK, :] = sd
            part = fold(sd[:, :BLK], jnp.maximum)
            top = part if top is None else jnp.maximum(top, part)
        top = jnp.max(top, axis=0, keepdims=True) * score_scale
        total = None
        dots = None
        for j in range(n):
            at = slice(j * BLK, (j + 1) * BLK)
            expo = jnp.exp2(sd_ref[at, :BLK] * score_scale - top)
            sd_ref[at, :BLK] = expo
            part = fold(expo, jnp.add)
            total = part if total is None else total + part
            part = fold(expo * sd_ref[at, BLK:], jnp.add)
            dots = part if dots is None else dots + part
        inv = 1.0 / jnp.sum(total, axis=0, keepdims=True)
        row_dot = jnp.sum(dots, axis=0, keepdims=True) * inv
        for j in range(n):
            at = slice(j * BLK, (j + 1) * BLK)
            prob = sd_ref[at, :BLK] * inv
            grad = prob * (sd_ref[at, BLK:] - row_dot)
            te = jnp.concatenate([grad.astype(BF), prob.astype(BF)], axis=1)
            te_ref[at, :] = te
            acc_ref[rows(picked[j]), :] += jnp.dot(te, pair, preferred_element_type=F32)
        kvt = jnp.concatenate([kvt_ref[rows(picked[j]), :] for j in range(n)], axis=1)
        out = jnp.dot(kvt, te_ref[:n * BLK, :], preferred_element_type=F32)
        dqt_ref[pl.ds(pl.multiple_of(i * HD, HD), HD), :] = out[:HD, :BLK] * HD ** -0.5
        ot_ref[:, rows(i)] = out[HD:, BLK:].astype(BF)

    @pl.loop(0, blocks)
    def _(i):
        count = count_ref[i]
        for n in range(2, MAXK + 1):
            @pl.when(count == n)
            def _():
                one_block(i, n)

    @pl.loop(0, blocks)
    def _(b):
        dkv_ref[rows(b), :] = (acc_ref[rows(b), :] * half_scale).astype(BF)

    @pl.loop(0, blocks // 2)
    def _(b):
        dq_ref[rows(b), :] = dqt_ref[rows(b), :].T.astype(BF)


def attention(adjacency, counts, q, g, kv):
    tokens = kv.shape[0]
    whole = pl.BlockSpec(memory_space=pltpu.VMEM)
    scalar = pl.BlockSpec(memory_space=pltpu.SMEM)
    return pl.pallas_call(
        attention_kernel,
        out_shape=(
            jax.ShapeDtypeStruct((tokens // 2, 2 * HD), BF),
            jax.ShapeDtypeStruct((HD, tokens), BF),
            jax.ShapeDtypeStruct((tokens, 2 * HD), BF),
        ),
        in_specs=[scalar, scalar, whole, whole, whole],
        out_specs=(whole, whole, whole),
        scratch_shapes=[
            pltpu.VMEM((tokens, 2 * HD), BF),
            pltpu.VMEM((tokens, 2 * HD), F32),
            pltpu.VMEM((tokens, 2 * HD), BF),
            pltpu.VMEM((tokens // 2, 2 * HD), F32),
            pltpu.VMEM((MAXK * BLK, 2 * BLK), F32),
            pltpu.VMEM((MAXK * BLK, 2 * BLK), BF),
        ],
        compiler_params=pltpu.CompilerParams(vmem_limit_bytes=48 << 20),
    )(adjacency, counts, q, g, kv)


def on_device(queries, keys, values, out_grad, out_weight, key_blocks, block_counts):
    q, kv, g, both = head_exchange(queries[0], keys[0], values[0], out_grad[0], out_weight)
    dq, ot, dkv = attention(
        key_blocks[0], block_counts[0], q.reshape(-1, 2 * HD), g.reshape(-1, 2 * HD),
        kv.reshape(-1, 2 * HD))
    dq, dkv, wo = tail_exchange(
        ot, dq.reshape(SEQ, BLK, 2 * HD), dkv.reshape(SEQ, ROWS, 2 * HD), both)
    query_grad, key_grad, value_grad, wo_grad = finish(dq, dkv, wo)
    return (query_grad[None], key_grad[None], value_grad[None], wo_grad)


def solution(mesh):
    return jax.shard_map(
        on_device,
        mesh=mesh,
        in_specs=(
            P("fsdp", "seq", None),
            P("fsdp", "seq", None),
            P("fsdp", "seq", None),
            P("fsdp", "seq", None),
            P("fsdp", None),
            P("fsdp", None, None),
            P("fsdp", None),
        ),
        out_specs=(
            P("fsdp", "seq", None),
            P("fsdp", "seq", None),
            P("fsdp", "seq", None),
            P("fsdp", None),
        ),
        check_vma=False,
    )
```

```python
import jax
import jax.numpy as jnp
from jax import lax
from jax.experimental import pallas as pl
from jax.experimental.pallas import tpu as pltpu
from jax.sharding import PartitionSpec as P

HEADS = 32
HD = 64
BLK = 128
MAXK = 10
NBLK = 64
GROUP = 2
LOG2E = 1.4426950408889634
SEQ = 32
SIDE = 4
CHIPS = 16
PLANES = 4
D = 2048
ROWS = 256
BF = jnp.bfloat16
F32 = jnp.float32
GROUPS = (10, 22, 28, 32)
PARTS = ((0, 768), (768, 640), (1408, 640))


def remote(src, dst, send_sem, recv_sem, **where):
    return pltpu.make_async_remote_copy(
        src_ref=src, dst_ref=dst, send_sem=send_sem, recv_sem=recv_sem,
        device_id=where, device_id_type=pl.DeviceIdType.MESH)


def local(src, dst, sem):
    return pltpu.make_async_copy(src, dst, sem)


def position():
    plane, member = lax.axis_index("fsdp"), lax.axis_index("seq")
    chip, core = lax.div(member, 2), lax.rem(member, 2)
    return plane, member, chip, core, lax.div(chip, SIDE), lax.rem(chip, SIDE)


def entry_barrier(plane, member):
    barrier = pltpu.get_barrier_semaphore()

    @pl.loop(1, SEQ)
    def _(k):
        pl.semaphore_signal(
            barrier, inc=1, device_id={"seq": lax.rem(member + k, SEQ)},
            device_id_type=pl.DeviceIdType.MESH)

    @pl.loop(1, PLANES)
    def _(k):
        pl.semaphore_signal(
            barrier, inc=1, device_id={"fsdp": lax.rem(plane + k, PLANES)},
            device_id_type=pl.DeviceIdType.MESH)

    pl.semaphore_wait(barrier, SEQ + PLANES - 2)


def owner(head):
    quarter, core, x = head // 8, head // SIDE % 2, head % SIDE
    return (x * SIDE + (x + quarter) % SIDE) * 2 + core


def traced_owner(quarter, core, x):
    return (x * SIDE + lax.rem(x + quarter, SIDE)) * 2 + core


def halves(one, two):
    return (jnp.concatenate([one[:, :HD], two[:, :HD]], axis=1),
            jnp.concatenate([one[:, HD:], two[:, HD:]], axis=1))


def head_kernel(q_ref, k_ref, v_ref, og_ref, w_ref, q_out, kv_out, g_out, both_out,
                q_pack, kv_pack, g_pack, both_ref, w_buf,
                q_send, kv_send, g_send, q_recv, kv_recv, g_recv,
                w_send, w_recv, w_own, both_send, both_recv, both_own):
    plane, member, chip, core, _, _ = position()
    up, down = lax.rem(plane + 1, PLANES), lax.rem(plane + 3, PLANES)
    far = lax.rem(plane + 2, PLANES)
    sibling = chip * 2 + 1 - core
    mine = pl.ds(pl.multiple_of(core * ROWS, ROWS), ROWS)
    w_mine = local(w_ref.at[mine], w_buf.at[plane], w_own.at[0])
    w_mine.start()
    both_mine = local(og_ref, both_ref.at[mine], w_own.at[1])
    both_mine.start()
    entry_barrier(plane, member)
    w_up = remote(w_ref.at[mine], w_buf.at[plane], w_send.at[0], w_recv.at[0], fsdp=up)
    w_down = remote(w_ref.at[mine], w_buf.at[plane], w_send.at[1], w_recv.at[1], fsdp=down)
    w_up.start()
    w_down.start()
    both_copy = remote(og_ref, both_ref.at[mine], both_send, both_recv, seq=sibling)
    both_copy.start()

    def send(block, head, out, slot, send_sem, recv_sem):
        @pl.when(head != member)
        def _():
            remote(block, out.at[slot], send_sem, recv_sem, seq=head).start()

        @pl.when(head == member)
        def _():
            local(block, out.at[slot], recv_sem).start()

    def sent(block, head, out, slot, send_sem, recv_sem):
        @pl.when(head != member)
        def _():
            remote(block, out.at[slot], send_sem, recv_sem, seq=head).wait_send()

    def pair_owner(j, e):
        return traced_owner(lax.div(j, 4), lax.rem(lax.div(j, 2), 2), lax.rem(j, 2) * 2 + e)

    @pl.loop(0, CHIPS)
    def _(k):
        j = lax.rem(chip + 5 * k, CHIPS)
        at = pl.ds(pl.multiple_of(j * 2 * HD, 2 * HD), 2 * HD)
        kv = halves(k_ref[:, at], v_ref[:, at])
        for e in range(2):
            to = pair_owner(j, e)
            kv_pack[to] = kv[e]
            send(kv_pack.at[to], to, kv_out, member, kv_send.at[to], kv_recv)

    @pl.loop(0, CHIPS)
    def _(k):
        j = lax.rem(chip + 5 * k, CHIPS)
        at = pl.ds(pl.multiple_of(j * 2 * HD, 2 * HD), 2 * HD)
        q = halves(q_ref[:BLK, at], q_ref[BLK:, at])
        for e in range(2):
            to = pair_owner(j, e)
            q_pack[to] = q[e]
            send(q_pack.at[to], to, q_out, member, q_send.at[to], q_recv)

    def project(which):
        for pair in range(2):
            grad = lax.dot_general(
                both_ref[...], w_buf[which, pair * BLK:(pair + 1) * BLK, :],
                (((1,), (1,)), ((), ())), preferred_element_type=F32).astype(BF)
            top = halves(grad[:BLK], grad[BLK:2 * BLK])
            low = halves(grad[2 * BLK:3 * BLK], grad[3 * BLK:])
            for e in range(2):
                slot = which * SIDE + pair * 2 + e
                head = traced_owner(which, core, pair * 2 + e)
                g_pack[slot, :BLK, :] = top[e]
                g_pack[slot, BLK:, :] = low[e]
                send(g_pack.at[slot], head, g_out, chip, g_send.at[slot], g_recv)

    w_mine.wait()
    both_mine.wait()
    both_copy.wait()
    both_write = local(both_ref, both_out, both_own)
    both_write.start()
    project(plane)
    w_up.wait()
    first = pl.ds(0, BLK)
    second = pl.ds(BLK, BLK)
    pass_up = remote(w_buf.at[down, first], w_buf.at[down, first], w_send.at[2], w_recv.at[2], fsdp=up)
    pass_up.start()
    w_down.wait()
    pass_down = remote(w_buf.at[up, second], w_buf.at[up, second], w_send.at[3], w_recv.at[3], fsdp=down)
    pass_down.start()
    project(down)
    project(up)
    pass_up.wait()
    pass_down.wait()
    project(far)
    both_write.wait()

    @pl.loop(0, SEQ)
    def _(d):
        sent(kv_pack.at[d], d, kv_out, member, kv_send.at[d], kv_recv)
        sent(q_pack.at[d], d, q_out, member, q_send.at[d], q_recv)

    @pl.loop(0, CHIPS)
    def _(slot):
        head = traced_owner(lax.div(slot, SIDE), core, lax.rem(slot, SIDE))
        sent(g_pack.at[slot], head, g_out, chip, g_send.at[slot], g_recv)

    local(kv_out, kv_out, kv_recv).wait()
    local(q_out, q_out, q_recv).wait()
    local(g_out, g_out, g_recv).wait()


def head_exchange(queries, keys, values, out_grad, out_weight):
    anyway = pl.BlockSpec(memory_space=pl.ANY)
    whole = pl.BlockSpec(memory_space=pltpu.VMEM)
    dma = pltpu.SemaphoreType.DMA
    return pl.pallas_call(
        head_kernel,
        out_shape=(
            jax.ShapeDtypeStruct((SEQ, BLK, 2 * HD), BF),
            jax.ShapeDtypeStruct((SEQ, ROWS, 2 * HD), BF),
            jax.ShapeDtypeStruct((CHIPS, ROWS, 2 * HD), BF),
            jax.ShapeDtypeStruct((2 * ROWS, D), BF),
        ),
        in_specs=[whole, whole, whole, whole, anyway],
        out_specs=(anyway, anyway, anyway, anyway),
        scratch_shapes=[
            pltpu.VMEM((SEQ, BLK, 2 * HD), BF),
            pltpu.VMEM((SEQ, ROWS, 2 * HD), BF),
            pltpu.VMEM((CHIPS, ROWS, 2 * HD), BF),
            pltpu.VMEM((2 * ROWS, D), BF),
            pltpu.VMEM((PLANES, ROWS, D), BF),
            dma((SEQ,)), dma((SEQ,)), dma((CHIPS,)), dma, dma, dma,
            dma((4,)), dma((4,)), dma((2,)), dma, dma, dma,
        ],
        compiler_params=pltpu.CompilerParams(
            collective_id=0, has_side_effects=True, vmem_limit_bytes=48 << 20),
    )(queries, keys, values, out_grad, out_weight)


def tail_kernel(ot_ref, dq_ref, dkv_ref, both_ref, dq_out, dkv_out, wo_out,
                o_buf, own_buf, *rest):
    bufs = [rest[6 * t:6 * t + 6] for t in range(3)]
    (o_send, dq_send, dkv_send, o_recv, dq_recv, dkv_recv, step_send, step_recv,
     wo_send, wo_recv, wo_own, pass_send, pass_recv) = rest[18:]
    plane, member, chip, core, x, y = position()
    entry_barrier(plane, member)
    slot = lax.rem(y + SIDE - x, SIDE) * SIDE + x

    def o_copy(q):
        at = pl.ds(pl.multiple_of(q * 2 * ROWS, 2 * ROWS), 2 * ROWS)
        return ot_ref.at[:, at], o_buf.at[slot]

    @pl.loop(0, CHIPS)
    def _(k):
        q = lax.rem(chip + 5 * k, CHIPS)
        to = q * 2 + core
        src, dst = o_copy(q)

        @pl.when(to != member)
        def _():
            remote(src, dst, o_send.at[q], o_recv, seq=to).start()

        @pl.when(to == member)
        def _():
            local(src, dst, o_recv).start()

    local(dq_ref.at[member], dq_out.at[member], dq_recv).start()
    local(dkv_ref.at[member], dkv_out.at[member], dkv_recv).start()

    def group(low, high):
        @pl.loop(low, high)
        def _(k):
            to = lax.rem(member + 9 * k, SEQ)
            remote(dkv_ref.at[to], dkv_out.at[member], dkv_send.at[to], dkv_recv, seq=to).start()
            remote(dq_ref.at[to], dq_out.at[member], dq_send.at[to], dq_recv, seq=to).start()

    group(1, GROUPS[0])
    local(o_buf, o_buf, o_recv).wait()

    def place(part, zq, value, at):
        buf = bufs[part][0]
        if part == 0:
            buf[zq, :, at] = value
            return
        for xq in range(SIDE):
            for yq in range(SIDE):
                piece = value[(xq * SIDE + yq) * 16:(xq * SIDE + yq + 1) * 16]
                if part == 1:
                    buf[xq, pl.ds(pl.multiple_of(yq * 64 + zq * 16, 16), 16), at] = piece
                else:
                    buf[yq, pl.ds(pl.multiple_of(zq * 64 + xq * 16, 16), 16), at] = piece

    axes = (("fsdp", plane), ("x", x), ("y", y))
    orders = ((0, 1, 2), (1, 2, 0), (2, 0, 1))

    def steps(part, stage):
        name, here = axes[orders[part][stage]]
        send_buf, recv_buf = bufs[part][2 * stage], bufs[part][2 * stage + 1]
        copies = []
        for k in range(1, SIDE):
            there = lax.rem(here + k, SIDE)
            if name == "fsdp":
                where = dict(fsdp=there)
            elif name == "x":
                where = dict(seq=(there * SIDE + y) * 2 + core)
            else:
                where = dict(seq=(x * SIDE + there) * 2 + core)
            copies.append(remote(
                send_buf.at[there], recv_buf.at[here],
                step_send.at[part, stage, k - 1], step_recv.at[part, stage, k - 1], **where))
        return copies, here, send_buf, recv_buf

    def start(part, stage):
        for copy in steps(part, stage)[0]:
            copy.start()

    def multiply(tiles, parts_of):
        @pl.loop(0, PLANES)
        def _(zq):
            lhs = o_buf[pl.ds(zq * SIDE, SIDE)].reshape(ROWS, 2 * ROWS)
            for tile in tiles:
                value = jnp.dot(
                    lhs, both_ref[:, tile * ROWS:(tile + 1) * ROWS],
                    preferred_element_type=F32).astype(BF)
                for half in range(2):
                    col = tile * ROWS + half * BLK
                    for part in parts_of:
                        base, width = PARTS[part]
                        if base <= col < base + width:
                            place(part, zq, value[:, half * BLK:(half + 1) * BLK],
                                  slice(col - base, col - base + BLK))

    multiply((0, 1, 2), (0,))
    start(0, 0)
    multiply((3, 4, 5), (1, 2))
    start(1, 0)
    multiply((6, 7), (2,))
    start(2, 0)
    group(GROUPS[0], GROUPS[1])

    for stage in range(3):
        for part in range(3):
            copies, here, send_buf, recv_buf = steps(part, stage)
            for copy in copies:
                copy.wait_recv()
            base, width = PARTS[part]
            rows = send_buf.shape[1]
            total = None
            for piece in range(max(1, rows // 64)):
                count = min(rows, 64)
                at = pl.ds(piece * count, count)
                total = send_buf[here, at, :].astype(F32)
                for k in range(1, SIDE):
                    total = total + recv_buf[lax.rem(here + k, SIDE), at, :].astype(F32)
                if stage == 2:
                    own_buf[:, base:base + width] = total.astype(BF)
                else:
                    next_buf = bufs[part][2 * stage + 2]
                    if rows == 256:
                        next_buf[piece] = total.astype(BF)
                    else:
                        for t in range(SIDE):
                            next_buf[t] = total[t * 16:(t + 1) * 16].astype(BF)
            if stage < 2:
                start(part, stage + 1)
        if stage < 2:
            group(GROUPS[stage + 1], GROUPS[stage + 2])

    def wo_rows(which, q):
        return wo_out.at[pl.ds(pl.multiple_of((which * CHIPS + q) * 16, 16), 16)]

    sibling = chip * 2 + 1 - core
    own = local(own_buf, wo_rows(core, chip), wo_own)
    own.start()

    @pl.loop(1, CHIPS)
    def _(k):
        q = lax.rem(chip + 5 * k, CHIPS)
        remote(own_buf, wo_rows(core, chip), wo_send.at[q], wo_recv.at[chip], seq=q * 2 + core).start()

    first = remote(own_buf, wo_rows(core, chip), pass_send.at[chip], pass_recv, seq=sibling)
    first.start()

    @pl.loop(1, CHIPS)
    def _(k):
        q = lax.rem(chip + 11 * k, CHIPS)
        remote(own_buf, wo_rows(core, q), wo_send.at[q], wo_recv.at[q], seq=q * 2 + core).wait_recv()
        remote(wo_rows(core, q), wo_rows(core, q), pass_send.at[q], pass_recv, seq=sibling).start()

    own.wait()
    other = pl.ds(pl.multiple_of((1 - core) * ROWS, ROWS), ROWS)
    local(wo_out.at[other], wo_out.at[other], pass_recv).wait()
    first.wait_send()

    @pl.loop(1, CHIPS)
    def _(k):
        q = lax.rem(chip + k, CHIPS)
        remote(own_buf, wo_rows(core, chip), wo_send.at[q], wo_recv.at[chip], seq=q * 2 + core).wait_send()
        remote(wo_rows(core, q), wo_rows(core, q), pass_send.at[q], pass_recv, seq=sibling).wait_send()

    @pl.loop(0, CHIPS)
    def _(q):
        to = q * 2 + core
        src, dst = o_copy(q)

        @pl.when(to != member)
        def _():
            remote(src, dst, o_send.at[q], o_recv, seq=to).wait_send()

    for stage in range(3):
        for part in range(3):
            for copy in steps(part, stage)[0]:
                copy.wait_send()

    @pl.loop(1, SEQ)
    def _(k):
        to = lax.rem(member + k, SEQ)
        remote(dkv_ref.at[to], dkv_out.at[member], dkv_send.at[to], dkv_recv, seq=to).wait_send()
        remote(dq_ref.at[to], dq_out.at[member], dq_send.at[to], dq_recv, seq=to).wait_send()

    local(dkv_out, dkv_out, dkv_recv).wait()
    local(dq_out, dq_out, dq_recv).wait()


def tail_exchange(ot, dq, dkv, both):
    anyway = pl.BlockSpec(memory_space=pl.ANY)
    whole = pl.BlockSpec(memory_space=pltpu.VMEM)
    dma = pltpu.SemaphoreType.DMA
    stages = []
    for _, width in PARTS:
        for rows in (256, 64, 16):
            stages += [pltpu.VMEM((SIDE, rows, width), BF)] * 2
    return pl.pallas_call(
        tail_kernel,
        out_shape=(
            jax.ShapeDtypeStruct((SEQ, BLK, 2 * HD), BF),
            jax.ShapeDtypeStruct((SEQ, ROWS, 2 * HD), BF),
            jax.ShapeDtypeStruct((2 * ROWS, D), BF),
        ),
        in_specs=[anyway, anyway, anyway, whole],
        out_specs=(anyway, anyway, anyway),
        scratch_shapes=[
            pltpu.VMEM((CHIPS, HD, 2 * ROWS), BF),
            pltpu.VMEM((16, D), BF),
            *stages,
            dma((CHIPS,)), dma((SEQ,)), dma((SEQ,)), dma, dma, dma,
            dma((3, 3, 3)), dma((3, 3, 3)),
            dma((CHIPS,)), dma((CHIPS,)), dma, dma((CHIPS,)), dma,
        ],
        compiler_params=pltpu.CompilerParams(
            collective_id=1, has_side_effects=True, vmem_limit_bytes=48 << 20),
    )(ot, dq, dkv, both)


def finish_kernel(dq_ref, dkv_ref, wo_ref, dq_out, dk_out, dv_out, wo_out):
    for j in range(HEADS // 2):
        at = slice(j * 2 * HD, (j + 1) * 2 * HD)
        one, two = dkv_ref[owner(2 * j)], dkv_ref[owner(2 * j + 1)]
        dk_out[:, at], dv_out[:, at] = halves(one, two)
        one, two = dq_ref[owner(2 * j)], dq_ref[owner(2 * j + 1)]
        dq_out[:BLK, at], dq_out[BLK:, at] = halves(one, two)
    for r in range(8):
        at = slice(r * 64, (r + 1) * 64)
        wo_out[at, :] = wo_ref[at, :].astype(F32)


def finish(dq, dkv, wo):
    whole = pl.BlockSpec(memory_space=pltpu.VMEM)
    shape = jax.ShapeDtypeStruct((ROWS, D), BF)
    return pl.pallas_call(
        finish_kernel,
        out_shape=(shape, shape, shape, jax.ShapeDtypeStruct(wo.shape, F32)),
        in_specs=[whole] * 3,
        out_specs=(whole,) * 4,
        compiler_params=pltpu.CompilerParams(vmem_limit_bytes=48 << 20),
    )(dq, dkv, wo)


def attention_kernel(adj_ref, count_ref, q_ref, g_ref, kv_ref, dq_ref, ot_ref, dkv_ref,
                     qg_ref, acc_ref, kvt_ref, dqt_ref, sd_ref, te_ref, list_ref, size_ref):
    blocks = kv_ref.shape[0] // BLK
    first = lax.broadcasted_iota(jnp.int32, (BLK, BLK), 1) < HD
    half_scale = jnp.where(first, HD ** -0.5, 1.0).astype(F32)
    score_scale = HD ** -0.5 * LOG2E

    def rows(b):
        return pl.ds(pl.multiple_of(b * BLK, BLK), BLK)

    def swap(value):
        return jnp.concatenate([value[:, HD:], value[:, :HD]], axis=1)

    @pl.loop(0, blocks // 8)
    def _(s):
        for t in range(8):
            b = s * 8 + t
            acc_ref[rows(b), :] = jnp.zeros((BLK, BLK), F32)
            kvt_ref[rows(b), :] = kv_ref[rows(b), :].T
        for t in range(4):
            b = s * 4 + t
            q, g = q_ref[rows(b), :], g_ref[rows(b), :]
            qg_ref[rows(2 * b), :] = jnp.where(first, q, swap(g))
            qg_ref[rows(2 * b + 1), :] = jnp.where(first, swap(q), g)

    for n in range(MAXK + 1):
        size_ref[n] = 0

    @pl.loop(0, blocks)
    def _(i):
        count = count_ref[i]
        filled = size_ref[count]
        list_ref[count, filled] = i
        size_ref[count] = filled + 1

    def fold(value, op):
        parts = [value[r * 8:(r + 1) * 8] for r in range(value.shape[0] // 8)]
        while len(parts) > 1:
            parts = [op(parts[t], parts[t + 1]) for t in range(0, len(parts) - 1, 2)] + (
                [parts[-1]] if len(parts) % 2 else [])
        return parts[0]

    def process(members, n):
        pairs, picked = [], []
        for i in members:
            qg = qg_ref[rows(i), :]
            zero = jnp.zeros_like(qg)
            pairs.append(jnp.concatenate(
                [jnp.where(first, qg, zero), jnp.where(first, zero, qg)], axis=0))
            picked.append([adj_ref[i, j] for j in range(n)])
        size = len(members)
        slots = [slice(j * BLK, (j + 1) * BLK) for j in range(n)]
        tops = []
        for m in range(size):
            top = None
            for j in range(n):
                sd = lax.dot_general(
                    kv_ref[rows(picked[m][j]), :], pairs[m], (((1,), (1,)), ((), ())),
                    preferred_element_type=F32)
                sd_ref[m, slots[j], :] = sd
                part = fold(sd[:, :BLK], jnp.maximum)
                top = part if top is None else jnp.maximum(top, part)
            tops.append(jnp.max(top, axis=0, keepdims=True) * score_scale)
        invs, row_dots = [], []
        for m in range(size):
            total = dots = None
            for j in range(n):
                expo = jnp.exp2(sd_ref[m, slots[j], :BLK] * score_scale - tops[m])
                sd_ref[m, slots[j], :BLK] = expo
                part = fold(expo, jnp.add)
                total = part if total is None else total + part
                part = fold(expo * sd_ref[m, slots[j], BLK:], jnp.add)
                dots = part if dots is None else dots + part
            inv = 1.0 / jnp.sum(total, axis=0, keepdims=True)
            invs.append(inv)
            row_dots.append(jnp.sum(dots, axis=0, keepdims=True) * inv)
        for m in range(size):
            for j in range(n):
                prob = sd_ref[m, slots[j], :BLK] * invs[m]
                grad = prob * (sd_ref[m, slots[j], BLK:] - row_dots[m])
                te = jnp.concatenate([grad.astype(BF), prob.astype(BF)], axis=1)
                te_ref[m, slots[j], :] = te
                acc_ref[rows(picked[m][j]), :] += jnp.dot(te, pairs[m], preferred_element_type=F32)
        for m in range(size):
            i = members[m]
            kvt = jnp.concatenate([kvt_ref[rows(picked[m][j]), :] for j in range(n)], axis=1)
            dq = jnp.dot(kvt[:HD], te_ref[m, :n * BLK, :BLK], preferred_element_type=F32)
            out = jnp.dot(kvt[HD:], te_ref[m, :n * BLK, BLK:], preferred_element_type=F32)
            dqt_ref[pl.ds(pl.multiple_of(i * HD, HD), HD), :] = dq * HD ** -0.5
            ot_ref[:, rows(i)] = out.astype(BF)

    for n in range(2, MAXK + 1):
        size = size_ref[n]
        whole = lax.div(size, GROUP)

        @pl.loop(0, whole)
        def _(t):
            process([list_ref[n, t * GROUP + m] for m in range(GROUP)], n)

        @pl.loop(whole * GROUP, size)
        def _(t):
            process([list_ref[n, t]], n)

    @pl.loop(0, blocks // 8)
    def _(s):
        for t in range(8):
            b = s * 8 + t
            dkv_ref[rows(b), :] = (acc_ref[rows(b), :] * half_scale).astype(BF)
        for t in range(4):
            b = s * 4 + t
            dq_ref[rows(b), :] = dqt_ref[rows(b), :].T.astype(BF)


def attention(adjacency, counts, q, g, kv):
    tokens = kv.shape[0]
    whole = pl.BlockSpec(memory_space=pltpu.VMEM)
    scalar = pl.BlockSpec(memory_space=pltpu.SMEM)
    return pl.pallas_call(
        attention_kernel,
        out_shape=(
            jax.ShapeDtypeStruct((tokens // 2, 2 * HD), BF),
            jax.ShapeDtypeStruct((HD, tokens), BF),
            jax.ShapeDtypeStruct((tokens, 2 * HD), BF),
        ),
        in_specs=[scalar, scalar, whole, whole, whole],
        out_specs=(whole, whole, whole),
        scratch_shapes=[
            pltpu.VMEM((tokens, 2 * HD), BF),
            pltpu.VMEM((tokens, 2 * HD), F32),
            pltpu.VMEM((tokens, 2 * HD), BF),
            pltpu.VMEM((tokens // 2, 2 * HD), F32),
            pltpu.VMEM((GROUP, MAXK * BLK, 2 * BLK), F32),
            pltpu.VMEM((GROUP, MAXK * BLK, 2 * BLK), BF),
            pltpu.SMEM((MAXK + 1, NBLK), jnp.int32),
            pltpu.SMEM((MAXK + 1,), jnp.int32),
        ],
        compiler_params=pltpu.CompilerParams(vmem_limit_bytes=48 << 20),
    )(adjacency, counts, q, g, kv)


def on_device(queries, keys, values, out_grad, out_weight, key_blocks, block_counts):
    q, kv, g, both = head_exchange(queries[0], keys[0], values[0], out_grad[0], out_weight)
    dq, ot, dkv = attention(
        key_blocks[0], block_counts[0], q.reshape(-1, 2 * HD), g.reshape(-1, 2 * HD),
        kv.reshape(-1, 2 * HD))
    dq, dkv, wo = tail_exchange(
        ot, dq.reshape(SEQ, BLK, 2 * HD), dkv.reshape(SEQ, ROWS, 2 * HD), both)
    query_grad, key_grad, value_grad, wo_grad = finish(dq, dkv, wo)
    return (query_grad[None], key_grad[None], value_grad[None], wo_grad)


def solution(mesh):
    return jax.shard_map(
        on_device,
        mesh=mesh,
        in_specs=(
            P("fsdp", "seq", None),
            P("fsdp", "seq", None),
            P("fsdp", "seq", None),
            P("fsdp", "seq", None),
            P("fsdp", None),
            P("fsdp", None, None),
            P("fsdp", None),
        ),
        out_specs=(
            P("fsdp", "seq", None),
            P("fsdp", "seq", None),
            P("fsdp", "seq", None),
            P("fsdp", None),
        ),
        check_vma=False,
    )
```

```python
import jax
import jax.numpy as jnp
from jax import lax
from jax.experimental import pallas as pl
from jax.experimental.pallas import tpu as pltpu
from jax.sharding import PartitionSpec as P

HEADS = 32
HD = 64
BLK = 128
MAXK = 10
NBLK = 64
GROUP = 2
LOG2E = 1.4426950408889634
SEQ = 32
SIDE = 4
CHIPS = 16
PLANES = 4
D = 2048
ROWS = 256
TRIPLE = BLK + ROWS
BF = jnp.bfloat16
F32 = jnp.float32
GROUPS = (20, 32, 32)
PARTS = ((0, 640), (640, 640), (1280, 384), (1664, 384))
ORDERS = ((0, 1, 2), (0, 2, 1), (1, 2, 0), (2, 0, 1))
STEPS = ((2, 0), (3, 0), (2, 1), (3, 1), (0, 0), (1, 0), (2, 2), (3, 2), (0, 1), (1, 1), (0, 2), (1, 2))


def remote(src, dst, send_sem, recv_sem, **where):
    return pltpu.make_async_remote_copy(
        src_ref=src, dst_ref=dst, send_sem=send_sem, recv_sem=recv_sem,
        device_id=where, device_id_type=pl.DeviceIdType.MESH)


def local(src, dst, sem):
    return pltpu.make_async_copy(src, dst, sem)


def position():
    plane, member = lax.axis_index("fsdp"), lax.axis_index("seq")
    chip, core = lax.div(member, 2), lax.rem(member, 2)
    return plane, member, chip, core, lax.div(chip, SIDE), lax.rem(chip, SIDE)


def entry_barrier(plane, member):
    barrier = pltpu.get_barrier_semaphore()

    @pl.loop(1, SEQ)
    def _(k):
        pl.semaphore_signal(
            barrier, inc=1, device_id={"seq": lax.rem(member + k, SEQ)},
            device_id_type=pl.DeviceIdType.MESH)

    @pl.loop(1, PLANES)
    def _(k):
        pl.semaphore_signal(
            barrier, inc=1, device_id={"fsdp": lax.rem(plane + k, PLANES)},
            device_id_type=pl.DeviceIdType.MESH)

    pl.semaphore_wait(barrier, SEQ + PLANES - 2)


def owner(head):
    quarter, core, x = head // 8, head // SIDE % 2, head % SIDE
    return (x * SIDE + (x + quarter) % SIDE) * 2 + core


def traced_owner(quarter, core, x):
    return (x * SIDE + lax.rem(x + quarter, SIDE)) * 2 + core


def halves(one, two):
    return (jnp.concatenate([one[:, :HD], two[:, :HD]], axis=1),
            jnp.concatenate([one[:, HD:], two[:, HD:]], axis=1))


def head_kernel(q_ref, k_ref, v_ref, og_ref, w_ref, all_out, g_out, both_out,
                q_buf, k_buf, v_buf, all_pack, g_pack, both_ref, w_buf,
                all_send, g_send, all_recv, g_recv, load_sem,
                w_send, w_recv, w_own, both_send, both_recv, both_own):
    plane, member, chip, core, _, _ = position()
    up, down = lax.rem(plane + 1, PLANES), lax.rem(plane + 3, PLANES)
    far = lax.rem(plane + 2, PLANES)
    sibling = chip * 2 + 1 - core
    mine = pl.ds(pl.multiple_of(core * ROWS, ROWS), ROWS)
    loads = [local(q_ref, q_buf, load_sem.at[0]), local(k_ref, k_buf, load_sem.at[1]),
             local(v_ref, v_buf, load_sem.at[2])]
    for load in loads:
        load.start()
    w_mine = local(w_ref.at[mine], w_buf.at[plane], w_own.at[0])
    w_mine.start()
    both_mine = local(og_ref, both_ref.at[mine], w_own.at[1])
    both_mine.start()
    entry_barrier(plane, member)
    w_up = remote(w_ref.at[mine], w_buf.at[plane], w_send.at[0], w_recv.at[0], fsdp=up)
    w_down = remote(w_ref.at[mine], w_buf.at[plane], w_send.at[1], w_recv.at[1], fsdp=down)
    w_up.start()
    w_down.start()
    both_copy = remote(og_ref, both_ref.at[mine], both_send, both_recv, seq=sibling)
    both_copy.start()

    def send(block, head, out, slot, send_sem, recv_sem):
        @pl.when(head != member)
        def _():
            remote(block, out.at[slot], send_sem, recv_sem, seq=head).start()

        @pl.when(head == member)
        def _():
            local(block, out.at[slot], recv_sem).start()

    def sent(block, head, out, slot, send_sem, recv_sem):
        @pl.when(head != member)
        def _():
            remote(block, out.at[slot], send_sem, recv_sem, seq=head).wait_send()

    def pair_owner(j, e):
        return traced_owner(lax.div(j, 4), lax.rem(lax.div(j, 2), 2), lax.rem(j, 2) * 2 + e)

    for load in loads:
        load.wait()

    @pl.loop(0, CHIPS)
    def _(k):
        j = lax.rem(chip + 5 * k, CHIPS)
        at = pl.ds(pl.multiple_of(j * 2 * HD, 2 * HD), 2 * HD)
        q = halves(q_buf[:BLK, at], q_buf[BLK:, at])
        kv = halves(k_buf[:, at], v_buf[:, at])
        for e in range(2):
            to = pair_owner(j, e)
            all_pack[to, :BLK] = q[e]
            all_pack[to, BLK:] = kv[e]
            send(all_pack.at[to], to, all_out, member, all_send.at[to], all_recv)

    def project(which):
        for pair in range(2):
            grad = lax.dot_general(
                both_ref[...], w_buf[which, pair * BLK:(pair + 1) * BLK, :],
                (((1,), (1,)), ((), ())), preferred_element_type=F32).astype(BF)
            top = halves(grad[:BLK], grad[BLK:2 * BLK])
            low = halves(grad[2 * BLK:3 * BLK], grad[3 * BLK:])
            for e in range(2):
                slot = which * SIDE + pair * 2 + e
                head = traced_owner(which, core, pair * 2 + e)
                g_pack[slot, :BLK, :] = top[e]
                g_pack[slot, BLK:, :] = low[e]
                send(g_pack.at[slot], head, g_out, chip, g_send.at[slot], g_recv)

    w_mine.wait()
    both_mine.wait()
    both_copy.wait()
    both_write = local(both_ref, both_out, both_own)
    both_write.start()
    project(plane)
    w_up.wait()
    first = pl.ds(0, BLK)
    second = pl.ds(BLK, BLK)
    pass_up = remote(w_buf.at[down, first], w_buf.at[down, first], w_send.at[2], w_recv.at[2], fsdp=up)
    pass_up.start()
    w_down.wait()
    pass_down = remote(w_buf.at[up, second], w_buf.at[up, second], w_send.at[3], w_recv.at[3], fsdp=down)
    pass_down.start()
    project(down)
    project(up)
    pass_up.wait()
    pass_down.wait()
    project(far)
    both_write.wait()

    @pl.loop(0, SEQ)
    def _(d):
        sent(all_pack.at[d], d, all_out, member, all_send.at[d], all_recv)

    @pl.loop(0, CHIPS)
    def _(slot):
        head = traced_owner(lax.div(slot, SIDE), core, lax.rem(slot, SIDE))
        sent(g_pack.at[slot], head, g_out, chip, g_send.at[slot], g_recv)

    local(all_out, all_out, all_recv).wait()
    local(g_out, g_out, g_recv).wait()


def head_exchange(queries, keys, values, out_grad, out_weight):
    anyway = pl.BlockSpec(memory_space=pl.ANY)
    dma = pltpu.SemaphoreType.DMA
    return pl.pallas_call(
        head_kernel,
        out_shape=(
            jax.ShapeDtypeStruct((SEQ, TRIPLE, 2 * HD), BF),
            jax.ShapeDtypeStruct((CHIPS, ROWS, 2 * HD), BF),
            jax.ShapeDtypeStruct((2 * ROWS, D), BF),
        ),
        in_specs=[pl.BlockSpec(memory_space=pltpu.HBM)] * 5,
        out_specs=(anyway, anyway, anyway),
        scratch_shapes=[
            pltpu.VMEM((ROWS, D), BF),
            pltpu.VMEM((ROWS, D), BF),
            pltpu.VMEM((ROWS, D), BF),
            pltpu.VMEM((SEQ, TRIPLE, 2 * HD), BF),
            pltpu.VMEM((CHIPS, ROWS, 2 * HD), BF),
            pltpu.VMEM((2 * ROWS, D), BF),
            pltpu.VMEM((PLANES, ROWS, D), BF),
            dma((SEQ,)), dma((CHIPS,)), dma, dma, dma((3,)),
            dma((4,)), dma((4,)), dma((2,)), dma, dma, dma,
        ],
        compiler_params=pltpu.CompilerParams(
            collective_id=0, has_side_effects=True, vmem_limit_bytes=60 << 20),
    )(queries, keys, values, out_grad, out_weight)


def tail_kernel(ot_ref, all_ref, both_in, all_out, wo_out,
                both_ref, o_buf, own_buf, *rest):
    parts = len(PARTS)
    bufs = [rest[6 * t:6 * t + 6] for t in range(parts)]
    (o_send, all_send, o_recv, all_recv, step_send, step_recv,
     wo_send, wo_recv, wo_own, pass_send, pass_recv, load_sem) = rest[6 * parts:]
    plane, member, chip, core, x, y = position()
    load = local(both_in, both_ref, load_sem)
    load.start()
    entry_barrier(plane, member)
    slot = lax.rem(y + SIDE - x, SIDE) * SIDE + x

    def o_copy(q):
        at = pl.ds(pl.multiple_of(q * 2 * ROWS, 2 * ROWS), 2 * ROWS)
        return ot_ref.at[:, at], o_buf.at[slot]

    @pl.loop(0, CHIPS)
    def _(k):
        q = lax.rem(chip + 5 * k, CHIPS)
        to = q * 2 + core
        src, dst = o_copy(q)

        @pl.when(to != member)
        def _():
            remote(src, dst, o_send.at[q], o_recv, seq=to).start()

        @pl.when(to == member)
        def _():
            local(src, dst, o_recv).start()

    local(all_ref.at[member], all_out.at[member], all_recv).start()

    def group(low, high):
        @pl.loop(low, high)
        def _(k):
            to = lax.rem(member + 9 * k, SEQ)
            remote(all_ref.at[to], all_out.at[member], all_send.at[to], all_recv, seq=to).start()

    group(1, GROUPS[0])
    load.wait()
    local(o_buf, o_buf, o_recv).wait()

    def place(part, zq, value, at):
        buf = bufs[part][0]
        if part == 0:
            buf[zq, :, at] = value
            return
        for xq in range(SIDE):
            for yq in range(SIDE):
                piece = value[(xq * SIDE + yq) * 16:(xq * SIDE + yq + 1) * 16]
                if part == 1:
                    buf[zq, yq * 64 + xq * 16:yq * 64 + xq * 16 + 16, at] = piece
                elif part == 2:
                    buf[xq, pl.ds(pl.multiple_of(yq * 64 + zq * 16, 16), 16), at] = piece
                else:
                    buf[yq, pl.ds(pl.multiple_of(zq * 64 + xq * 16, 16), 16), at] = piece

    axes = (("fsdp", plane), ("x", x), ("y", y))

    def steps(part, stage):
        name, here = axes[ORDERS[part][stage]]
        send_buf, recv_buf = bufs[part][2 * stage], bufs[part][2 * stage + 1]
        copies = []
        for k in range(1, SIDE):
            there = lax.rem(here + k, SIDE)
            if name == "fsdp":
                where = dict(fsdp=there)
            elif name == "x":
                where = dict(seq=(there * SIDE + y) * 2 + core)
            else:
                where = dict(seq=(x * SIDE + there) * 2 + core)
            copies.append(remote(
                send_buf.at[there], recv_buf.at[here],
                step_send.at[part, stage, k - 1], step_recv.at[part, stage, k - 1], **where))
        return copies, here, send_buf, recv_buf

    def start(part, stage):
        for copy in steps(part, stage)[0]:
            copy.start()

    def multiply(tiles, parts_of):
        @pl.loop(0, PLANES)
        def _(zq):
            lhs = o_buf[pl.ds(zq * SIDE, SIDE)].reshape(ROWS, 2 * ROWS)
            for tile in tiles:
                value = jnp.dot(
                    lhs, both_ref[:, tile * ROWS:(tile + 1) * ROWS],
                    preferred_element_type=F32).astype(BF)
                for half in range(2):
                    col = tile * ROWS + half * BLK
                    for part in parts_of:
                        base, width = PARTS[part]
                        if base <= col < base + width:
                            place(part, zq, value[:, half * BLK:(half + 1) * BLK],
                                  slice(col - base, col - base + BLK))

    multiply((0, 1, 2), (0, 1))
    start(0, 0)
    multiply((3, 4), (1,))
    start(1, 0)
    multiply((5, 6), (2, 3))
    start(2, 0)
    multiply((7,), (3,))
    start(3, 0)
    group(GROUPS[0], GROUPS[1])

    for part, stage in STEPS:
        copies, here, send_buf, recv_buf = steps(part, stage)
        for copy in copies:
            copy.wait_recv()
        base, width = PARTS[part]
        rows = send_buf.shape[1]
        for piece in range(max(1, rows // 64)):
            count = min(rows, 64)
            at = pl.ds(piece * count, count)
            total = send_buf[here, at, :].astype(F32)
            for k in range(1, SIDE):
                total = total + recv_buf[lax.rem(here + k, SIDE), at, :].astype(F32)
            if stage == 2:
                own_buf[:, base:base + width] = total.astype(BF)
            else:
                next_buf = bufs[part][2 * stage + 2]
                if rows == 256:
                    next_buf[piece] = total.astype(BF)
                else:
                    for t in range(SIDE):
                        next_buf[t] = total[t * 16:(t + 1) * 16].astype(BF)
        if stage < 2:
            start(part, stage + 1)
        if (part, stage) == (3, 0):
            group(GROUPS[1], GROUPS[2])

    def wo_rows(which, q):
        return wo_out.at[pl.ds(pl.multiple_of((which * CHIPS + q) * 16, 16), 16)]

    sibling = chip * 2 + 1 - core
    own = local(own_buf, wo_rows(core, chip), wo_own)
    own.start()

    @pl.loop(1, CHIPS)
    def _(k):
        q = lax.rem(chip + 5 * k, CHIPS)
        remote(own_buf, wo_rows(core, chip), wo_send.at[q], wo_recv.at[chip], seq=q * 2 + core).start()

    def pass_copy(row):
        rows = wo_out.at[pl.ds(pl.multiple_of((core * CHIPS + row * SIDE) * 16, 64), 64)]
        return remote(rows, rows, pass_send.at[row], pass_recv, seq=sibling)

    own.wait()
    for k in range(SIDE):
        row = lax.rem(x + k, SIDE)
        for t in range(SIDE):
            q = row * SIDE + lax.rem(y + t, SIDE)
            if k == 0 and t == 0:
                continue
            remote(own_buf, wo_rows(core, q), wo_send.at[q], wo_recv.at[q], seq=q * 2 + core).wait_recv()
        pass_copy(row).start()

    other = pl.ds(pl.multiple_of((1 - core) * ROWS, ROWS), ROWS)
    local(wo_out.at[other], wo_out.at[other], pass_recv).wait()

    @pl.loop(0, SIDE)
    def _(row):
        pass_copy(row).wait_send()

    @pl.loop(1, CHIPS)
    def _(k):
        q = lax.rem(chip + k, CHIPS)
        remote(own_buf, wo_rows(core, chip), wo_send.at[q], wo_recv.at[chip], seq=q * 2 + core).wait_send()

    @pl.loop(0, CHIPS)
    def _(q):
        to = q * 2 + core
        src, dst = o_copy(q)

        @pl.when(to != member)
        def _():
            remote(src, dst, o_send.at[q], o_recv, seq=to).wait_send()

    for part, stage in STEPS:
        for copy in steps(part, stage)[0]:
            copy.wait_send()

    @pl.loop(1, SEQ)
    def _(k):
        to = lax.rem(member + k, SEQ)
        remote(all_ref.at[to], all_out.at[member], all_send.at[to], all_recv, seq=to).wait_send()

    local(all_out, all_out, all_recv).wait()


def tail_exchange(ot, grads, both):
    anyway = pl.BlockSpec(memory_space=pl.ANY)
    dma = pltpu.SemaphoreType.DMA
    stages = []
    for _, width in PARTS:
        for rows in (256, 64, 16):
            stages += [pltpu.VMEM((SIDE, rows, width), BF)] * 2
    return pl.pallas_call(
        tail_kernel,
        out_shape=(
            jax.ShapeDtypeStruct((SEQ, TRIPLE, 2 * HD), BF),
            jax.ShapeDtypeStruct((2 * ROWS, D), BF),
        ),
        in_specs=[anyway, anyway, anyway],
        out_specs=(anyway, anyway),
        scratch_shapes=[
            pltpu.VMEM((2 * ROWS, D), BF),
            pltpu.VMEM((CHIPS, HD, 2 * ROWS), BF),
            pltpu.VMEM((16, D), BF),
            *stages,
            dma((CHIPS,)), dma((SEQ,)), dma, dma,
            dma((len(PARTS), 3, 3)), dma((len(PARTS), 3, 3)),
            dma((CHIPS,)), dma((CHIPS,)), dma, dma((SIDE,)), dma, dma,
        ],
        compiler_params=pltpu.CompilerParams(
            collective_id=1, has_side_effects=True, vmem_limit_bytes=60 << 20),
    )(ot, grads, both)


def finish_kernel(dq_ref, dkv_ref, wo_ref, dq_out, dk_out, dv_out, wo_out):
    step = pl.program_id(0)
    for j in range(HEADS // 2):
        at = slice(j * 2 * HD, (j + 1) * 2 * HD)
        one, two = owner(2 * j), owner(2 * j + 1)
        dk_out[:, at], dv_out[:, at] = halves(dkv_ref[one], dkv_ref[two])
        low, high = halves(dq_ref[one], dq_ref[two])
        dq_out[:, at] = jnp.where(step < 2, low, high)
    wo_out[...] = wo_ref[...].astype(F32)


def finish(grads, wo):
    rows = ROWS // 4
    packed = (SEQ, rows, 2 * HD)
    shape = jax.ShapeDtypeStruct((ROWS, D), BF)
    block = pl.BlockSpec((rows, D), lambda r: (r, 0))
    term = pl.BlockSpec((2 * rows, D), lambda r: (r, 0))
    return pl.pallas_call(
        finish_kernel,
        grid=(4,),
        out_shape=(shape, shape, shape, jax.ShapeDtypeStruct(wo.shape, F32)),
        in_specs=[
            pl.BlockSpec(packed, lambda r: (0, lax.rem(r, 2), 0)),
            pl.BlockSpec(packed, lambda r: (0, r + 2, 0)),
            term,
        ],
        out_specs=(block, block, block, term),
        compiler_params=pltpu.CompilerParams(vmem_limit_bytes=60 << 20),
    )(grads, grads, wo)


def attention_kernel(adj_in, count_in, all_ref, g_ref, ot_ref, grads_ref,
                     qg_ref, acc_ref, kvt_ref, dqt_ref, sd_ref, te_ref, list_ref, size_ref,
                     adj_ref, count_ref, table_sem):
    blocks = ot_ref.shape[1] // BLK
    tables = [pltpu.make_async_copy(adj_in.at[0], adj_ref, table_sem.at[0]),
              pltpu.make_async_copy(count_in.at[0], count_ref, table_sem.at[1])]
    for table in tables:
        table.start()
    first = lax.broadcasted_iota(jnp.int32, (BLK, BLK), 1) < HD
    half_scale = jnp.where(first, HD ** -0.5, 1.0).astype(F32)
    score_scale = HD ** -0.5 * LOG2E

    def rows(b):
        return pl.ds(pl.multiple_of(b * BLK, BLK), BLK)

    def kv_rows(b):
        return pl.ds(pl.multiple_of((b + lax.div(b, 2) + 1) * BLK, BLK), BLK)

    def q_rows(b):
        return pl.ds(pl.multiple_of(b * TRIPLE, BLK), BLK)

    def swap(value):
        return jnp.concatenate([value[:, HD:], value[:, :HD]], axis=1)

    @pl.loop(0, blocks // 8)
    def _(s):
        for t in range(8):
            b = s * 8 + t
            acc_ref[rows(b), :] = jnp.zeros((BLK, BLK), F32)
            kvt_ref[rows(b), :] = all_ref[kv_rows(b), :].T
        for t in range(4):
            b = s * 4 + t
            q, g = all_ref[q_rows(b), :], g_ref[rows(b), :]
            qg_ref[rows(2 * b), :] = jnp.where(first, q, swap(g))
            qg_ref[rows(2 * b + 1), :] = jnp.where(first, swap(q), g)

    for n in range(MAXK + 1):
        size_ref[n] = 0
    for table in tables:
        table.wait()

    @pl.loop(0, blocks)
    def _(i):
        count = count_ref[i]
        filled = size_ref[count]
        list_ref[count, filled] = i
        size_ref[count] = filled + 1

    def fold(value, op):
        parts = [value[r * 8:(r + 1) * 8] for r in range(value.shape[0] // 8)]
        while len(parts) > 1:
            parts = [op(parts[t], parts[t + 1]) for t in range(0, len(parts) - 1, 2)] + (
                [parts[-1]] if len(parts) % 2 else [])
        return parts[0]

    def process(members, n):
        pairs, picked = [], []
        for i in members:
            qg = qg_ref[rows(i), :]
            zero = jnp.zeros_like(qg)
            pairs.append(jnp.concatenate(
                [jnp.where(first, qg, zero), jnp.where(first, zero, qg)], axis=0))
            picked.append([adj_ref[i, j] for j in range(n)])
        size = len(members)
        slots = [slice(j * BLK, (j + 1) * BLK) for j in range(n)]
        tops = []
        for m in range(size):
            top = None
            for j in range(n):
                sd = lax.dot_general(
                    all_ref[kv_rows(picked[m][j]), :], pairs[m], (((1,), (1,)), ((), ())),
                    preferred_element_type=F32)
                sd_ref[m, slots[j], :] = sd
                part = fold(sd[:, :BLK], jnp.maximum)
                top = part if top is None else jnp.maximum(top, part)
            tops.append(jnp.max(top, axis=0, keepdims=True) * score_scale)
        invs, row_dots = [], []
        for m in range(size):
            total = dots = None
            for j in range(n):
                expo = jnp.exp2(sd_ref[m, slots[j], :BLK] * score_scale - tops[m])
                sd_ref[m, slots[j], :BLK] = expo
                part = fold(expo, jnp.add)
                total = part if total is None else total + part
                part = fold(expo * sd_ref[m, slots[j], BLK:], jnp.add)
                dots = part if dots is None else dots + part
            inv = 1.0 / jnp.sum(total, axis=0, keepdims=True)
            invs.append(inv)
            row_dots.append(jnp.sum(dots, axis=0, keepdims=True) * inv)
        for m in range(size):
            for j in range(n):
                prob = sd_ref[m, slots[j], :BLK] * invs[m]
                grad = prob * (sd_ref[m, slots[j], BLK:] - row_dots[m])
                te = jnp.concatenate([grad.astype(BF), prob.astype(BF)], axis=1)
                te_ref[m, slots[j], :] = te
                acc_ref[rows(picked[m][j]), :] += jnp.dot(te, pairs[m], preferred_element_type=F32)
        for m in range(size):
            i = members[m]
            kvt = jnp.concatenate([kvt_ref[rows(picked[m][j]), :] for j in range(n)], axis=1)
            dq = jnp.dot(kvt[:HD], te_ref[m, :n * BLK, :BLK], preferred_element_type=F32)
            out = jnp.dot(kvt[HD:], te_ref[m, :n * BLK, BLK:], preferred_element_type=F32)
            dqt_ref[pl.ds(pl.multiple_of(i * HD, HD), HD), :] = dq * HD ** -0.5
            ot_ref[:, rows(i)] = out.astype(BF)

    for n in range(2, MAXK + 1):
        size = size_ref[n]
        whole = lax.div(size, GROUP)

        @pl.loop(0, whole)
        def _(t):
            process([list_ref[n, t * GROUP + m] for m in range(GROUP)], n)

        @pl.loop(whole * GROUP, size)
        def _(t):
            process([list_ref[n, t]], n)

    @pl.loop(0, blocks // 8)
    def _(s):
        for t in range(8):
            b = s * 8 + t
            grads_ref[kv_rows(b), :] = (acc_ref[rows(b), :] * half_scale).astype(BF)
        for t in range(4):
            b = s * 4 + t
            grads_ref[q_rows(b), :] = dqt_ref[rows(b), :].T.astype(BF)


def attention(adjacency, counts, tokens_in, g):
    tokens = 2 * g.shape[0]
    whole = pl.BlockSpec(memory_space=pltpu.VMEM)
    scalar = pl.BlockSpec(memory_space=pltpu.HBM)
    return pl.pallas_call(
        attention_kernel,
        out_shape=(
            jax.ShapeDtypeStruct((HD, tokens), BF),
            jax.ShapeDtypeStruct(tokens_in.shape, BF),
        ),
        in_specs=[scalar, scalar, whole, whole],
        out_specs=(whole, whole),
        scratch_shapes=[
            pltpu.VMEM((tokens, 2 * HD), BF),
            pltpu.VMEM((tokens, 2 * HD), F32),
            pltpu.VMEM((tokens, 2 * HD), BF),
            pltpu.VMEM((tokens // 2, 2 * HD), F32),
            pltpu.VMEM((GROUP, MAXK * BLK, 2 * BLK), F32),
            pltpu.VMEM((GROUP, MAXK * BLK, 2 * BLK), BF),
            pltpu.SMEM((MAXK + 1, NBLK), jnp.int32),
            pltpu.SMEM((MAXK + 1,), jnp.int32),
            pltpu.SMEM((NBLK, MAXK), jnp.int32),
            pltpu.SMEM((NBLK,), jnp.int32),
            pltpu.SemaphoreType.DMA((2,)),
        ],
        compiler_params=pltpu.CompilerParams(vmem_limit_bytes=60 << 20),
    )(adjacency, counts, tokens_in, g)


def on_device(queries, keys, values, out_grad, out_weight, key_blocks, block_counts):
    tokens_in, g, both = head_exchange(queries[0], keys[0], values[0], out_grad[0], out_weight)
    ot, grads = attention(
        key_blocks, block_counts, tokens_in.reshape(-1, 2 * HD), g.reshape(-1, 2 * HD))
    grads, wo = tail_exchange(ot, grads.reshape(SEQ, TRIPLE, 2 * HD), both)
    query_grad, key_grad, value_grad, wo_grad = finish(grads, wo)
    return (query_grad[None], key_grad[None], value_grad[None], wo_grad)


def solution(mesh):
    return jax.shard_map(
        on_device,
        mesh=mesh,
        in_specs=(
            P("fsdp", "seq", None),
            P("fsdp", "seq", None),
            P("fsdp", "seq", None),
            P("fsdp", "seq", None),
            P("fsdp", None),
            P("fsdp", None, None),
            P("fsdp", None),
        ),
        out_specs=(
            P("fsdp", "seq", None),
            P("fsdp", "seq", None),
            P("fsdp", "seq", None),
            P("fsdp", None),
        ),
        check_vma=False,
    )
```

```python
import jax
import jax.numpy as jnp
from jax import lax
from jax.experimental import pallas as pl
from jax.experimental.pallas import tpu as pltpu
from jax.sharding import PartitionSpec as P

HEADS = 32
HD = 64
BLK = 128
MAXK = 10
NBLK = 64
SPANS = (3, 2, 1)
LOG2E = 1.4426950408889634
SEQ = 32
SIDE = 4
CHIPS = 16
PLANES = 4
D = 2048
ROWS = 256
TRIPLE = BLK + ROWS
BF = jnp.bfloat16
F32 = jnp.float32
GROUPS = (20, 32, 32)
PARTS = ((0, 768), (768, 768), (1536, 256), (1792, 256))
ORDERS = ((0, 1, 2), (0, 2, 1), (1, 2, 0), (2, 0, 1))
STEPS = ((2, 0), (3, 0), (2, 1), (3, 1), (0, 0), (1, 0), (2, 2), (3, 2), (0, 1), (1, 1), (0, 2), (1, 2))


def remote(src, dst, send_sem, recv_sem, **where):
    return pltpu.make_async_remote_copy(
        src_ref=src, dst_ref=dst, send_sem=send_sem, recv_sem=recv_sem,
        device_id=where, device_id_type=pl.DeviceIdType.MESH)


def local(src, dst, sem):
    return pltpu.make_async_copy(src, dst, sem)


def position():
    plane, member = lax.axis_index("fsdp"), lax.axis_index("seq")
    chip, core = lax.div(member, 2), lax.rem(member, 2)
    return plane, member, chip, core, lax.div(chip, SIDE), lax.rem(chip, SIDE)


def entry_barrier(plane, member):
    barrier = pltpu.get_barrier_semaphore()

    @pl.loop(1, SEQ)
    def _(k):
        pl.semaphore_signal(
            barrier, inc=1, device_id={"seq": lax.rem(member + k, SEQ)},
            device_id_type=pl.DeviceIdType.MESH)

    @pl.loop(1, PLANES)
    def _(k):
        pl.semaphore_signal(
            barrier, inc=1, device_id={"fsdp": lax.rem(plane + k, PLANES)},
            device_id_type=pl.DeviceIdType.MESH)

    pl.semaphore_wait(barrier, SEQ + PLANES - 2)


def owner(head):
    quarter, core, x = head // 8, head // SIDE % 2, head % SIDE
    return (x * SIDE + (x + quarter) % SIDE) * 2 + core


def traced_owner(quarter, core, x):
    return (x * SIDE + lax.rem(x + quarter, SIDE)) * 2 + core


def halves(one, two):
    return (jnp.concatenate([one[:, :HD], two[:, :HD]], axis=1),
            jnp.concatenate([one[:, HD:], two[:, HD:]], axis=1))


def head_kernel(q_ref, k_ref, v_ref, og_ref, w_ref, all_out, g_out, both_out,
                q_buf, k_buf, v_buf, all_pack, g_pack, both_ref, w_buf,
                all_send, g_send, all_recv, g_recv, load_sem,
                w_send, w_recv, w_own, both_send, both_recv, both_own):
    plane, member, chip, core, _, _ = position()
    up, down = lax.rem(plane + 1, PLANES), lax.rem(plane + 3, PLANES)
    far = lax.rem(plane + 2, PLANES)
    sibling = chip * 2 + 1 - core
    mine = pl.ds(pl.multiple_of(core * ROWS, ROWS), ROWS)
    loads = [local(q_ref, q_buf, load_sem.at[0]), local(k_ref, k_buf, load_sem.at[1]),
             local(v_ref, v_buf, load_sem.at[2])]
    for load in loads:
        load.start()
    w_mine = local(w_ref.at[mine], w_buf.at[plane], w_own.at[0])
    w_mine.start()
    both_mine = local(og_ref, both_ref.at[mine], w_own.at[1])
    both_mine.start()
    entry_barrier(plane, member)
    w_up = remote(w_ref.at[mine], w_buf.at[plane], w_send.at[0], w_recv.at[0], fsdp=up)
    w_down = remote(w_ref.at[mine], w_buf.at[plane], w_send.at[1], w_recv.at[1], fsdp=down)
    w_up.start()
    w_down.start()
    both_copy = remote(og_ref, both_ref.at[mine], both_send, both_recv, seq=sibling)
    both_copy.start()

    def send(block, head, out, slot, send_sem, recv_sem):
        @pl.when(head != member)
        def _():
            remote(block, out.at[slot], send_sem, recv_sem, seq=head).start()

        @pl.when(head == member)
        def _():
            local(block, out.at[slot], recv_sem).start()

    def sent(block, head, out, slot, send_sem, recv_sem):
        @pl.when(head != member)
        def _():
            remote(block, out.at[slot], send_sem, recv_sem, seq=head).wait_send()

    def pair_owner(j, e):
        return traced_owner(lax.div(j, 4), lax.rem(lax.div(j, 2), 2), lax.rem(j, 2) * 2 + e)

    for load in loads:
        load.wait()

    @pl.loop(0, CHIPS)
    def _(k):
        j = lax.rem(chip + 5 * k, CHIPS)
        at = pl.ds(pl.multiple_of(j * 2 * HD, 2 * HD), 2 * HD)
        q = halves(q_buf[:BLK, at], q_buf[BLK:, at])
        kv = halves(k_buf[:, at], v_buf[:, at])
        for e in range(2):
            to = pair_owner(j, e)
            all_pack[to, :BLK] = q[e]
            all_pack[to, BLK:] = kv[e]
            send(all_pack.at[to], to, all_out, member, all_send.at[to], all_recv)

    def project(which):
        for pair in range(2):
            grad = lax.dot_general(
                both_ref[...], w_buf[which, pair * BLK:(pair + 1) * BLK, :],
                (((1,), (1,)), ((), ())), preferred_element_type=F32).astype(BF)
            top = halves(grad[:BLK], grad[BLK:2 * BLK])
            low = halves(grad[2 * BLK:3 * BLK], grad[3 * BLK:])
            for e in range(2):
                slot = which * SIDE + pair * 2 + e
                head = traced_owner(which, core, pair * 2 + e)
                g_pack[slot, :BLK, :] = top[e]
                g_pack[slot, BLK:, :] = low[e]
                send(g_pack.at[slot], head, g_out, chip, g_send.at[slot], g_recv)

    w_mine.wait()
    both_mine.wait()
    both_copy.wait()
    both_write = local(both_ref, both_out, both_own)
    both_write.start()
    project(plane)
    w_up.wait()
    first = pl.ds(0, BLK)
    second = pl.ds(BLK, BLK)
    pass_up = remote(w_buf.at[down, first], w_buf.at[down, first], w_send.at[2], w_recv.at[2], fsdp=up)
    pass_up.start()
    w_down.wait()
    pass_down = remote(w_buf.at[up, second], w_buf.at[up, second], w_send.at[3], w_recv.at[3], fsdp=down)
    pass_down.start()
    project(down)
    project(up)
    pass_up.wait()
    pass_down.wait()
    project(far)
    both_write.wait()

    @pl.loop(0, SEQ)
    def _(d):
        sent(all_pack.at[d], d, all_out, member, all_send.at[d], all_recv)

    @pl.loop(0, CHIPS)
    def _(slot):
        head = traced_owner(lax.div(slot, SIDE), core, lax.rem(slot, SIDE))
        sent(g_pack.at[slot], head, g_out, chip, g_send.at[slot], g_recv)

    local(all_out, all_out, all_recv).wait()
    local(g_out, g_out, g_recv).wait()


def head_exchange(queries, keys, values, out_grad, out_weight):
    anyway = pl.BlockSpec(memory_space=pl.ANY)
    dma = pltpu.SemaphoreType.DMA
    return pl.pallas_call(
        head_kernel,
        out_shape=(
            jax.ShapeDtypeStruct((SEQ, TRIPLE, 2 * HD), BF),
            jax.ShapeDtypeStruct((CHIPS, ROWS, 2 * HD), BF),
            jax.ShapeDtypeStruct((2 * ROWS, D), BF),
        ),
        in_specs=[pl.BlockSpec(memory_space=pltpu.HBM)] * 5,
        out_specs=(anyway, anyway, anyway),
        scratch_shapes=[
            pltpu.VMEM((ROWS, D), BF),
            pltpu.VMEM((ROWS, D), BF),
            pltpu.VMEM((ROWS, D), BF),
            pltpu.VMEM((SEQ, TRIPLE, 2 * HD), BF),
            pltpu.VMEM((CHIPS, ROWS, 2 * HD), BF),
            pltpu.VMEM((2 * ROWS, D), BF),
            pltpu.VMEM((PLANES, ROWS, D), BF),
            dma((SEQ,)), dma((CHIPS,)), dma, dma, dma((3,)),
            dma((4,)), dma((4,)), dma((2,)), dma, dma, dma,
        ],
        compiler_params=pltpu.CompilerParams(
            collective_id=0, has_side_effects=True, vmem_limit_bytes=60 << 20),
    )(queries, keys, values, out_grad, out_weight)


def tail_kernel(ot_ref, all_ref, both_in, all_out, wo_out,
                both_ref, o_buf, own_buf, *rest):
    parts = len(PARTS)
    bufs = [rest[6 * t:6 * t + 6] for t in range(parts)]
    (o_send, all_send, o_recv, all_recv, step_send, step_recv,
     wo_send, wo_recv, wo_own, pass_send, pass_recv, load_sem) = rest[6 * parts:]
    plane, member, chip, core, x, y = position()
    load = local(both_in, both_ref, load_sem)
    load.start()
    entry_barrier(plane, member)
    slot = lax.rem(y + SIDE - x, SIDE) * SIDE + x

    def o_copy(q):
        at = pl.ds(pl.multiple_of(q * 2 * ROWS, 2 * ROWS), 2 * ROWS)
        return ot_ref.at[:, at], o_buf.at[slot]

    @pl.loop(0, CHIPS)
    def _(k):
        q = lax.rem(chip + 5 * k, CHIPS)
        to = q * 2 + core
        src, dst = o_copy(q)

        @pl.when(to != member)
        def _():
            remote(src, dst, o_send.at[q], o_recv, seq=to).start()

        @pl.when(to == member)
        def _():
            local(src, dst, o_recv).start()

    local(all_ref.at[member], all_out.at[member], all_recv).start()

    def group(low, high):
        @pl.loop(low, high)
        def _(k):
            to = lax.rem(member + 9 * k, SEQ)
            remote(all_ref.at[to], all_out.at[member], all_send.at[to], all_recv, seq=to).start()

    group(1, GROUPS[0])
    load.wait()
    local(o_buf, o_buf, o_recv).wait()

    def place(part, zq, value, at):
        buf = bufs[part][0]
        if part == 0:
            buf[zq, :, at] = value
            return
        for xq in range(SIDE):
            for yq in range(SIDE):
                piece = value[(xq * SIDE + yq) * 16:(xq * SIDE + yq + 1) * 16]
                if part == 1:
                    buf[zq, yq * 64 + xq * 16:yq * 64 + xq * 16 + 16, at] = piece
                elif part == 2:
                    buf[xq, pl.ds(pl.multiple_of(yq * 64 + zq * 16, 16), 16), at] = piece
                else:
                    buf[yq, pl.ds(pl.multiple_of(zq * 64 + xq * 16, 16), 16), at] = piece

    axes = (("fsdp", plane), ("x", x), ("y", y))

    def steps(part, stage):
        name, here = axes[ORDERS[part][stage]]
        send_buf, recv_buf = bufs[part][2 * stage], bufs[part][2 * stage + 1]
        copies = []
        for k in range(1, SIDE):
            there = lax.rem(here + k, SIDE)
            if name == "fsdp":
                where = dict(fsdp=there)
            elif name == "x":
                where = dict(seq=(there * SIDE + y) * 2 + core)
            else:
                where = dict(seq=(x * SIDE + there) * 2 + core)
            copies.append(remote(
                send_buf.at[there], recv_buf.at[here],
                step_send.at[part, stage, k - 1], step_recv.at[part, stage, k - 1], **where))
        return copies, here, send_buf, recv_buf

    def start(part, stage):
        for copy in steps(part, stage)[0]:
            copy.start()

    def multiply(tiles, parts_of):
        @pl.loop(0, PLANES)
        def _(zq):
            lhs = o_buf[pl.ds(zq * SIDE, SIDE)].reshape(ROWS, 2 * ROWS)
            for tile in tiles:
                value = jnp.dot(
                    lhs, both_ref[:, tile * ROWS:(tile + 1) * ROWS],
                    preferred_element_type=F32).astype(BF)
                for half in range(2):
                    col = tile * ROWS + half * BLK
                    for part in parts_of:
                        base, width = PARTS[part]
                        if base <= col < base + width:
                            place(part, zq, value[:, half * BLK:(half + 1) * BLK],
                                  slice(col - base, col - base + BLK))

    multiply((0, 1, 2), (0,))
    start(0, 0)
    multiply((3, 4, 5), (1,))
    start(1, 0)
    multiply((6,), (2,))
    start(2, 0)
    multiply((7,), (3,))
    start(3, 0)
    group(GROUPS[0], GROUPS[1])

    for part, stage in STEPS:
        copies, here, send_buf, recv_buf = steps(part, stage)
        for copy in copies:
            copy.wait_recv()
        base, width = PARTS[part]
        rows = send_buf.shape[1]
        for piece in range(max(1, rows // 64)):
            count = min(rows, 64)
            at = pl.ds(piece * count, count)
            total = send_buf[here, at, :].astype(F32)
            for k in range(1, SIDE):
                total = total + recv_buf[lax.rem(here + k, SIDE), at, :].astype(F32)
            if stage == 2:
                own_buf[:, base:base + width] = total.astype(BF)
            else:
                next_buf = bufs[part][2 * stage + 2]
                if rows == 256:
                    next_buf[piece] = total.astype(BF)
                else:
                    for t in range(SIDE):
                        next_buf[t] = total[t * 16:(t + 1) * 16].astype(BF)
        if stage < 2:
            start(part, stage + 1)
        if (part, stage) == (3, 0):
            group(GROUPS[1], GROUPS[2])

    def wo_rows(which, q):
        return wo_out.at[pl.ds(pl.multiple_of((which * CHIPS + q) * 16, 16), 16)]

    sibling = chip * 2 + 1 - core
    own = local(own_buf, wo_rows(core, chip), wo_own)
    own.start()

    @pl.loop(1, CHIPS)
    def _(k):
        q = lax.rem(chip + 5 * k, CHIPS)
        remote(own_buf, wo_rows(core, chip), wo_send.at[q], wo_recv.at[chip], seq=q * 2 + core).start()

    def pass_copy(row):
        rows = wo_out.at[pl.ds(pl.multiple_of((core * CHIPS + row * SIDE) * 16, 64), 64)]
        return remote(rows, rows, pass_send.at[row], pass_recv, seq=sibling)

    own.wait()
    for k in range(SIDE):
        row = lax.rem(x + k, SIDE)
        for t in range(SIDE):
            q = row * SIDE + lax.rem(y + t, SIDE)
            if k == 0 and t == 0:
                continue
            remote(own_buf, wo_rows(core, q), wo_send.at[q], wo_recv.at[q], seq=q * 2 + core).wait_recv()
        pass_copy(row).start()

    other = pl.ds(pl.multiple_of((1 - core) * ROWS, ROWS), ROWS)
    local(wo_out.at[other], wo_out.at[other], pass_recv).wait()

    @pl.loop(0, SIDE)
    def _(row):
        pass_copy(row).wait_send()

    @pl.loop(1, CHIPS)
    def _(k):
        q = lax.rem(chip + k, CHIPS)
        remote(own_buf, wo_rows(core, chip), wo_send.at[q], wo_recv.at[chip], seq=q * 2 + core).wait_send()

    @pl.loop(0, CHIPS)
    def _(q):
        to = q * 2 + core
        src, dst = o_copy(q)

        @pl.when(to != member)
        def _():
            remote(src, dst, o_send.at[q], o_recv, seq=to).wait_send()

    for part, stage in STEPS:
        for copy in steps(part, stage)[0]:
            copy.wait_send()

    @pl.loop(1, SEQ)
    def _(k):
        to = lax.rem(member + k, SEQ)
        remote(all_ref.at[to], all_out.at[member], all_send.at[to], all_recv, seq=to).wait_send()

    local(all_out, all_out, all_recv).wait()


def tail_exchange(ot, grads, both):
    anyway = pl.BlockSpec(memory_space=pl.ANY)
    dma = pltpu.SemaphoreType.DMA
    stages = []
    for _, width in PARTS:
        for rows in (256, 64, 16):
            stages += [pltpu.VMEM((SIDE, rows, width), BF)] * 2
    return pl.pallas_call(
        tail_kernel,
        out_shape=(
            jax.ShapeDtypeStruct((SEQ, TRIPLE, 2 * HD), BF),
            jax.ShapeDtypeStruct((2 * ROWS, D), BF),
        ),
        in_specs=[anyway, anyway, anyway],
        out_specs=(anyway, anyway),
        scratch_shapes=[
            pltpu.VMEM((2 * ROWS, D), BF),
            pltpu.VMEM((CHIPS, HD, 2 * ROWS), BF),
            pltpu.VMEM((16, D), BF),
            *stages,
            dma((CHIPS,)), dma((SEQ,)), dma, dma,
            dma((len(PARTS), 3, 3)), dma((len(PARTS), 3, 3)),
            dma((CHIPS,)), dma((CHIPS,)), dma, dma((SIDE,)), dma, dma,
        ],
        compiler_params=pltpu.CompilerParams(
            collective_id=1, has_side_effects=True, vmem_limit_bytes=60 << 20),
    )(ot, grads, both)


def finish_kernel(dq_ref, dkv_ref, wo_ref, dq_out, dk_out, dv_out, wo_out):
    step = pl.program_id(0)
    for j in range(HEADS // 2):
        at = slice(j * 2 * HD, (j + 1) * 2 * HD)
        one, two = owner(2 * j), owner(2 * j + 1)
        dk_out[:, at], dv_out[:, at] = halves(dkv_ref[one], dkv_ref[two])
        low, high = halves(dq_ref[one], dq_ref[two])
        dq_out[:, at] = jnp.where(lax.rem(step, 2) == 0, low, high)
    wo_out[...] = wo_ref[...].astype(F32)


def finish(grads, wo):
    rows = ROWS // 4
    packed = (SEQ, rows, 2 * HD)
    shape = jax.ShapeDtypeStruct((ROWS, D), BF)
    block = pl.BlockSpec((rows, D), lambda r: (r, 0))
    term = pl.BlockSpec((2 * rows, D), lambda r: (r, 0))
    turned = pl.BlockSpec((rows, D), lambda r: (lax.rem(r, 2) * 2 + lax.div(r, 2), 0))
    return pl.pallas_call(
        finish_kernel,
        grid=(4,),
        out_shape=(shape, shape, shape, jax.ShapeDtypeStruct(wo.shape, F32)),
        in_specs=[
            pl.BlockSpec(packed, lambda r: (0, lax.div(r, 2), 0)),
            pl.BlockSpec(packed, lambda r: (0, r + 2, 0)),
            term,
        ],
        out_specs=(turned, block, block, term),
        compiler_params=pltpu.CompilerParams(vmem_limit_bytes=60 << 20),
    )(grads, grads, wo)


def attention_kernel(adj_in, count_in, all_ref, g_ref, ot_ref, grads_ref,
                     qg_ref, acc_ref, kvt_ref, dqt_ref, sd_ref, te_ref, list_ref, size_ref,
                     adj_ref, count_ref, table_sem):
    blocks = ot_ref.shape[1] // BLK
    tables = [pltpu.make_async_copy(adj_in.at[0], adj_ref, table_sem.at[0]),
              pltpu.make_async_copy(count_in.at[0], count_ref, table_sem.at[1])]
    for table in tables:
        table.start()
    first = lax.broadcasted_iota(jnp.int32, (BLK, BLK), 1) < HD
    half_scale = jnp.where(first, HD ** -0.5, 1.0).astype(F32)
    score_scale = HD ** -0.5 * LOG2E

    def rows(b):
        return pl.ds(pl.multiple_of(b * BLK, BLK), BLK)

    def kv_rows(b):
        return pl.ds(pl.multiple_of((b + lax.div(b, 2) + 1) * BLK, BLK), BLK)

    def q_rows(b):
        return pl.ds(pl.multiple_of(b * TRIPLE, BLK), BLK)

    def swap(value):
        return jnp.concatenate([value[:, HD:], value[:, :HD]], axis=1)

    @pl.loop(0, blocks // 8)
    def _(s):
        for t in range(8):
            b = s * 8 + t
            acc_ref[rows(b), :] = jnp.zeros((BLK, BLK), F32)
            kvt_ref[rows(b), :] = all_ref[kv_rows(b), :].T
        for t in range(4):
            b = s * 4 + t
            q, g = all_ref[q_rows(b), :], g_ref[rows(b), :]
            qg_ref[rows(2 * b), :] = jnp.where(first, q, swap(g))
            qg_ref[rows(2 * b + 1), :] = jnp.where(first, swap(q), g)

    for n in range(MAXK + 1):
        size_ref[n] = 0
    for table in tables:
        table.wait()

    @pl.loop(0, blocks)
    def _(i):
        count = count_ref[i]
        filled = size_ref[count]
        list_ref[count, filled] = i
        size_ref[count] = filled + 1

    def fold(value, op):
        parts = [value[r * 8:(r + 1) * 8] for r in range(value.shape[0] // 8)]
        while len(parts) > 1:
            parts = [op(parts[t], parts[t + 1]) for t in range(0, len(parts) - 1, 2)] + (
                [parts[-1]] if len(parts) % 2 else [])
        return parts[0]

    def process(members, n):
        pairs, picked = [], []
        for i in members:
            qg = qg_ref[rows(i), :]
            zero = jnp.zeros_like(qg)
            pairs.append(jnp.concatenate(
                [jnp.where(first, qg, zero), jnp.where(first, zero, qg)], axis=0))
            picked.append([adj_ref[i, j] for j in range(n)])
        size = len(members)
        slots = [slice(j * BLK, (j + 1) * BLK) for j in range(n)]
        tops = []
        for m in range(size):
            top = None
            for j in range(n):
                sd = lax.dot_general(
                    all_ref[kv_rows(picked[m][j]), :], pairs[m], (((1,), (1,)), ((), ())),
                    preferred_element_type=F32)
                sd_ref[m, slots[j], :] = sd
                part = fold(sd[:, :BLK], jnp.maximum)
                top = part if top is None else jnp.maximum(top, part)
            tops.append(jnp.max(top, axis=0, keepdims=True) * score_scale)
        invs, row_dots = [], []
        for m in range(size):
            total = dots = None
            for j in range(n):
                expo = jnp.exp2(sd_ref[m, slots[j], :BLK] * score_scale - tops[m])
                sd_ref[m, slots[j], :BLK] = expo
                part = fold(expo, jnp.add)
                total = part if total is None else total + part
                part = fold(expo * sd_ref[m, slots[j], BLK:], jnp.add)
                dots = part if dots is None else dots + part
            inv = 1.0 / jnp.sum(total, axis=0, keepdims=True)
            invs.append(inv)
            row_dots.append(jnp.sum(dots, axis=0, keepdims=True) * inv)
        for m in range(size):
            for j in range(n):
                prob = sd_ref[m, slots[j], :BLK] * invs[m]
                grad = prob * (sd_ref[m, slots[j], BLK:] - row_dots[m])
                te = jnp.concatenate([grad.astype(BF), prob.astype(BF)], axis=1)
                te_ref[m, slots[j], :] = te
                acc_ref[rows(picked[m][j]), :] += jnp.dot(te, pairs[m], preferred_element_type=F32)
        for m in range(size):
            i = members[m]
            kvt = jnp.concatenate([kvt_ref[rows(picked[m][j]), :] for j in range(n)], axis=1)
            dq = jnp.dot(kvt[:HD], te_ref[m, :n * BLK, :BLK], preferred_element_type=F32)
            out = jnp.dot(kvt[HD:], te_ref[m, :n * BLK, BLK:], preferred_element_type=F32)
            dqt_ref[pl.ds(pl.multiple_of(i * HD, HD), HD), :] = dq * HD ** -0.5
            ot_ref[:, rows(i)] = out.astype(BF)

    for n in range(2, MAXK + 1):
        size = size_ref[n]
        done = 0
        for span in SPANS:
            steps = lax.div(size - done, span)

            @pl.loop(0, steps)
            def _(t, n=n, span=span, done=done):
                process([list_ref[n, done + t * span + m] for m in range(span)], n)

            done = done + steps * span

    @pl.loop(0, blocks // 8)
    def _(s):
        for t in range(8):
            b = s * 8 + t
            grads_ref[kv_rows(b), :] = (acc_ref[rows(b), :] * half_scale).astype(BF)
        for t in range(4):
            b = s * 4 + t
            grads_ref[q_rows(b), :] = dqt_ref[rows(b), :].T.astype(BF)


def attention(adjacency, counts, tokens_in, g):
    tokens = 2 * g.shape[0]
    whole = pl.BlockSpec(memory_space=pltpu.VMEM)
    scalar = pl.BlockSpec(memory_space=pltpu.HBM)
    return pl.pallas_call(
        attention_kernel,
        out_shape=(
            jax.ShapeDtypeStruct((HD, tokens), BF),
            jax.ShapeDtypeStruct(tokens_in.shape, BF),
        ),
        in_specs=[scalar, scalar, whole, whole],
        out_specs=(whole, whole),
        scratch_shapes=[
            pltpu.VMEM((tokens, 2 * HD), BF),
            pltpu.VMEM((tokens, 2 * HD), F32),
            pltpu.VMEM((tokens, 2 * HD), BF),
            pltpu.VMEM((tokens // 2, 2 * HD), F32),
            pltpu.VMEM((SPANS[0], MAXK * BLK, 2 * BLK), F32),
            pltpu.VMEM((SPANS[0], MAXK * BLK, 2 * BLK), BF),
            pltpu.SMEM((MAXK + 1, NBLK), jnp.int32),
            pltpu.SMEM((MAXK + 1,), jnp.int32),
            pltpu.SMEM((NBLK, MAXK), jnp.int32),
            pltpu.SMEM((NBLK,), jnp.int32),
            pltpu.SemaphoreType.DMA((2,)),
        ],
        compiler_params=pltpu.CompilerParams(vmem_limit_bytes=60 << 20),
    )(adjacency, counts, tokens_in, g)


def on_device(queries, keys, values, out_grad, out_weight, key_blocks, block_counts):
    tokens_in, g, both = head_exchange(queries[0], keys[0], values[0], out_grad[0], out_weight)
    ot, grads = attention(
        key_blocks, block_counts, tokens_in.reshape(-1, 2 * HD), g.reshape(-1, 2 * HD))
    grads, wo = tail_exchange(ot, grads.reshape(SEQ, TRIPLE, 2 * HD), both)
    query_grad, key_grad, value_grad, wo_grad = finish(grads, wo)
    return (query_grad[None], key_grad[None], value_grad[None], wo_grad)


def solution(mesh):
    return jax.shard_map(
        on_device,
        mesh=mesh,
        in_specs=(
            P("fsdp", "seq", None),
            P("fsdp", "seq", None),
            P("fsdp", "seq", None),
            P("fsdp", "seq", None),
            P("fsdp", None),
            P("fsdp", None, None),
            P("fsdp", None),
        ),
        out_specs=(
            P("fsdp", "seq", None),
            P("fsdp", "seq", None),
            P("fsdp", "seq", None),
            P("fsdp", None),
        ),
        check_vma=False,
    )
```
